128 devices in a mesh: ctx: 32 (over y, z_hi, x), ch: 4 (over z_lo, core).
Axes of the slice: x: 4, y: 4, z: 4 (z_hi: 2, z_lo: 2; z = z_hi * 2 + z_lo), core: 2. Of those that a mesh axis runs over, the one named last changes fastest.
Arguments:
- signal: bfloat16 [128, 524288], P('ch', 'ctx'), parts along dimension 0, may hold values from -6 to 6
- filter_taps: float32 [128, 524288], P('ch', 'ctx'), parts along dimension 0, may hold values from -0.0078125 to 0.0078125
- gate_values: bfloat16 [128, 524288], P('ch', 'ctx'), parts along dimension 0, may hold values from -6 to 6
- skip_gain: float32 [128], P('ch'), parts along dimension 0, may hold values from -4 to 4
Outputs:
- gated_output: bfloat16 [128, 524288], P('ch', 'ctx'), parts along dimension 0
The draws below stay inside these ranges and needn't reach their ends.
There are 4 independent parts, one for each index of `ch`. The reference program is written for one: setup_inputs(seed, part) draws one part's arguments, and reference() takes and returns one part's arrays. A program takes and returns all parts, laid end to end along the dimension named above; each array names one. Nothing has to cross between parts.
All inputs are finite; a program needn't handle non-finite values.
Results may differ from the reference program's by a relative error of at most 0.001.
Values sent between devices are 32-bit elements; how exact they have to be, the bound alone decides.
No kernel may reach another device: no remote copies, remote signals or barrier semaphores. Data moves between devices by JAX's collectives and lax.ppermute only.
A program may use at most 128 MiB of HBM per device.

```python
import jax
import jax.numpy as jnp

CHANNELS = 32
SEQ = 524288


def block_levels(key, extent, split, least, top_value):
    gain = 1.0
    for position, shards_of in split:
        draws = jax.random.uniform(jax.random.fold_in(jax.random.fold_in(key, 6), position), (shards_of,), jnp.float32, least / len(split), top_value / len(split))
        gain = gain * jnp.repeat(jnp.exp(draws), extent[position] // shards_of).reshape((-1,) + (1,) * (len(extent) - 1 - position))
    return gain


def bell_draw(stream_key, extent, scale, most, shards=(), kind=jnp.bfloat16):
    gain = block_levels(stream_key, extent, shards, -0.22, 0.18) if shards else 1.0
    values = jax.random.normal(stream_key, extent, jnp.float32) * scale * gain
    return jnp.minimum(jnp.maximum(values, -most), most).astype(kind)


def setup_inputs(seed: int = 0, part: int = 0) -> dict:
    streams_of = jax.random.split(jax.random.key(seed), 5)
    own_keys = jax.random.split(jax.random.fold_in(streams_of[4], part), 5)
    signal = bell_draw(own_keys[0], (CHANNELS, SEQ), 1.0, 6.0, ((1, 32),))
    filter_taps = bell_draw(own_keys[1], (CHANNELS, SEQ), SEQ ** -0.5, 0.0078125, ((1, 32),), jnp.float32)
    gate_values = bell_draw(own_keys[2], (CHANNELS, SEQ), 1.0, 6.0, ((1, 32),))
    skip_gain = bell_draw(own_keys[3], (CHANNELS,), 1.0, 4.0, (), jnp.float32)
    return {"signal": signal, "filter_taps": filter_taps, "gate_values": gate_values, "skip_gain": skip_gain}


def reference(signal, filter_taps, gate_values, skip_gain):
    length = signal.shape[1]
    inputs = signal.astype(jnp.float32)
    spectrum = jnp.fft.rfft(inputs, n=2 * length, axis=1) * jnp.fft.rfft(filter_taps, n=2 * length, axis=1)
    long_conv = jnp.fft.irfft(spectrum, n=2 * length, axis=1)[:, :length].astype(jnp.float32)
    gated = gate_values.astype(jnp.float32) * (long_conv + skip_gain[:, None] * inputs)
    return gated.astype(jnp.bfloat16)
```

```python
import math

import jax
import jax.numpy as jnp
import numpy as np
from jax import lax
from jax.experimental import pallas as pl
from jax.experimental.pallas import tpu as pltpu
from jax.sharding import PartitionSpec as P

F32 = jnp.float32
BF16 = jnp.bfloat16
ROWS = 256
MIDS = 16
LANES = 128
TOTAL = ROWS * MIDS * LANES


def wave(product, period):
    angle = 2.0 * np.pi * (product % period) / period
    return np.cos(angle), np.sin(angle)


def halves_of(table):
    upper = table.astype(jnp.bfloat16)
    lower = (table - upper.astype(np.float64)).astype(jnp.bfloat16)
    return upper, lower


def host_tables():
    n1 = np.arange(ROWS, dtype=np.int64)
    k1 = np.arange(ROWS, dtype=np.int64)
    cos1, sin1 = wave((4 * k1[:, None] + 1) * n1[None, :], 4 * ROWS)
    first = np.concatenate([cos1, -sin1], axis=0)
    lane = np.arange(LANES, dtype=np.int64)
    cos3, sin3 = wave(lane[:, None] * lane[None, :], LANES)
    third = np.block([[cos3, -sin3], [sin3, cos3]])
    k2 = np.arange(MIDS, dtype=np.int64)
    cos2, sin2 = wave(k2[:, None] * lane[None, :], MIDS * LANES)
    mid = np.stack([cos2, -sin2]).astype(np.float32)
    return first, third, mid


def row_twiddle():
    shape = (MIDS, ROWS, LANES)
    position = lax.broadcasted_iota(jnp.int32, shape, 0) * LANES + lax.broadcasted_iota(jnp.int32, shape, 2)
    product = position * (4 * lax.broadcasted_iota(jnp.int32, shape, 1) + 1)
    angle = (2.0 * math.pi / (4 * TOTAL)) * (product % (4 * TOTAL)).astype(F32)
    return jnp.cos(angle), -jnp.sin(angle)


def split(values):
    upper = values.astype(BF16)
    return upper, (values - upper.astype(F32)).astype(BF16)


def dot(left, right):
    return jnp.dot(left, right, preferred_element_type=F32)


def times(a, b):
    return a[0] * b[0] - a[1] * b[1], a[0] * b[1] + a[1] * b[0]


def conj_times(a, b):
    return a[0] * b[0] + a[1] * b[1], a[1] * b[0] - a[0] * b[1]


def four_point(v, sign):
    s0 = (v[0][0] + v[2][0], v[0][1] + v[2][1])
    d0 = (v[0][0] - v[2][0], v[0][1] - v[2][1])
    s1 = (v[1][0] + v[3][0], v[1][1] + v[3][1])
    d1 = (v[1][0] - v[3][0], v[1][1] - v[3][1])
    r1 = (-sign * d1[1], sign * d1[0]) if sign > 0 else (d1[1], -d1[0])
    return [
        (s0[0] + s1[0], s0[1] + s1[1]),
        (d0[0] + r1[0], d0[1] + r1[1]),
        (s0[0] - s1[0], s0[1] - s1[1]),
        (d0[0] - r1[0], d0[1] - r1[1]),
    ]


def turn(v, step, sign):
    step = step % 16
    if step == 0:
        return v
    root = math.sqrt(0.5)
    if step == 2:
        if sign < 0:
            return ((v[0] + v[1]) * root, (v[1] - v[0]) * root)
        return ((v[0] - v[1]) * root, (v[1] + v[0]) * root)
    if step == 4:
        return (v[1], -v[0]) if sign < 0 else (-v[1], v[0])
    c, s = math.cos(2 * math.pi * step / 16), sign * math.sin(2 * math.pi * step / 16)
    return (v[0] * c - v[1] * s, v[0] * s + v[1] * c)


def sixteen_point(v, sign):
    columns = [four_point([v[4 * p + q] for p in range(4)], sign) for q in range(4)]
    out = [None] * 16
    for r in range(4):
        row = four_point([turn(columns[q][r], q * r, sign) for q in range(4)], sign)
        for s in range(4):
            out[r + 4 * s] = row[s]
    return out


def pack_kernel(src_ref, out_ref):
    channels, length = src_ref.shape
    for group in range(channels // 8):
        for row in range(length // LANES):
            value = src_ref[pl.ds(8 * group, 8), pl.ds(row * LANES, LANES)].astype(F32)
            place = (row % MIDS) * (LANES // MIDS) + row // MIDS
            out_ref[pl.ds(8 * group * LANES + place, 8, stride=LANES), :] = value


def pack(values):
    channels, length = values.shape
    block = 16
    return pl.pallas_call(
        pack_kernel,
        grid=(channels // block,),
        in_specs=[pl.BlockSpec((block, length), lambda i: (i, 0))],
        out_specs=pl.BlockSpec((block * LANES, LANES), lambda i: (i, 0)),
        out_shape=jax.ShapeDtypeStruct((channels * LANES, LANES), F32),
        name="pack",
    )(values)


def forward_rows(src_ref, first_hi, first_lo, tw_re, tw_im, work_re, work_im, exact):
    def step(pair, carry):
        even = src_ref[:, 2 * pair].reshape(ROWS, LANES)
        odd = src_ref[:, 2 * pair + 1].reshape(ROWS, LANES)
        values = jnp.concatenate([even, odd], axis=1)
        if exact:
            upper = values.astype(BF16)
            out = dot(first_hi[...], upper) + dot(first_lo[...], upper)
        else:
            upper, lower = split(values)
            out = dot(first_hi[...], upper) + (dot(first_lo[...], upper) + dot(first_hi[...], lower))
        for side in range(2):
            lanes = slice(side * LANES, (side + 1) * LANES)
            mid = 2 * pair + side
            re, im = times((out[:ROWS, lanes], out[ROWS:, lanes]), (tw_re[mid], tw_im[mid]))
            work_re[mid] = re
            work_im[mid] = im
        return carry

    lax.fori_loop(0, MIDS // 2, step, 0)


def forward_mids(mid_ref, work_re, work_im):
    def step(group, carry):
        rows = pl.ds(pl.multiple_of(group * 8, 8), 8)
        out = sixteen_point([(work_re[m, rows], work_im[m, rows]) for m in range(MIDS)], -1)
        for k in range(MIDS):
            value = out[k]
            if k:
                value = times(value, (mid_ref[0, k : k + 1], mid_ref[1, k : k + 1]))
            work_re[k, rows] = value[0]
            work_im[k, rows] = value[1]
        return carry

    lax.fori_loop(0, ROWS // 8, step, 0)


def lane_stage(values, third_hi, third_lo):
    upper, lower = split(values)
    return dot(upper, third_hi[...]) + (dot(upper, third_lo[...]) + dot(lower, third_hi[...]))


def taps_kernel(src_ref, first_hi, first_lo, third_hi, third_lo, mid_ref, tw_re, tw_im, out_ref, work_re, work_im):
    forward_rows(src_ref, first_hi, first_lo, tw_re, tw_im, work_re, work_im, False)
    forward_mids(mid_ref, work_re, work_im)

    def step(k, carry):
        values = jnp.concatenate([work_re[k], work_im[k]], axis=1)
        out_ref[k] = lane_stage(values, third_hi, third_lo)
        return carry

    lax.fori_loop(0, MIDS, step, 0)


def signal_kernel(
    src_ref, spec_ref, first_hi, first_lo, back_hi, back_lo, third_hi, third_lo, undo_hi, undo_lo,
    mid_ref, tw_re, tw_im, out_ref, work_re, work_im,
):
    forward_rows(src_ref, first_hi, first_lo, tw_re, tw_im, work_re, work_im, True)
    forward_mids(mid_ref, work_re, work_im)

    def step(k, carry):
        values = jnp.concatenate([work_re[k], work_im[k]], axis=1)
        seen = lane_stage(values, third_hi, third_lo)
        spec = spec_ref[k]
        prod = times((seen[:, :LANES], seen[:, LANES:]), (spec[:, :LANES], spec[:, LANES:]))
        back = lane_stage(jnp.concatenate(prod, axis=1), undo_hi, undo_lo)
        work_re[k] = back[:, :LANES]
        work_im[k] = back[:, LANES:]
        return carry

    lax.fori_loop(0, MIDS, step, 0)

    def mids(group, carry):
        rows = pl.ds(pl.multiple_of(group * 8, 8), 8)
        values = []
        for k in range(MIDS):
            value = (work_re[k, rows], work_im[k, rows])
            if k:
                value = conj_times(value, (mid_ref[0, k : k + 1], mid_ref[1, k : k + 1]))
            values.append(value)
        out = sixteen_point(values, 1)
        for m in range(MIDS):
            re, im = conj_times(out[m], (tw_re[m, rows], tw_im[m, rows]))
            work_re[m, rows] = re
            work_im[m, rows] = im
        return carry

    lax.fori_loop(0, ROWS // 8, mids, 0)

    def last(pair, carry):
        values = jnp.concatenate(
            [
                jnp.concatenate([work_re[2 * pair], work_im[2 * pair]], axis=0),
                jnp.concatenate([work_re[2 * pair + 1], work_im[2 * pair + 1]], axis=0),
            ],
            axis=1,
        )
        upper, lower = split(values)
        out = dot(back_hi[...], upper) + (dot(back_lo[...], upper) + dot(back_hi[...], lower))
        blocks = src_ref.shape[0]
        out_ref[:, 2 * pair] = out[:, :LANES].reshape(blocks, ROWS // blocks, LANES)
        out_ref[:, 2 * pair + 1] = out[:, LANES:].reshape(blocks, ROWS // blocks, LANES)
        return carry

    lax.fori_loop(0, MIDS // 2, last, 0)


def gate_kernel(conv_ref, signal_ref, gate_ref, skip_ref, out_ref):
    channels, length = signal_ref.shape
    for group in range(channels // 8):
        skip = skip_ref[pl.ds(8 * group, 8), :]
        for row in range(length // LANES):
            where = (pl.ds(8 * group, 8), pl.ds(row * LANES, LANES))
            place = (row % MIDS) * (LANES // MIDS) + row // MIDS
            conv = conv_ref[pl.ds(8 * group * LANES + place, 8, stride=LANES), :]
            total = conv + skip * signal_ref[where].astype(F32)
            out_ref[where] = (gate_ref[where].astype(F32) * total).astype(BF16)


def gate(conv, signal, gate_values, skip_gain):
    channels, length = signal.shape
    block = 16
    skip = jnp.broadcast_to(skip_gain[:, None], (channels, LANES))
    line = pl.BlockSpec((block, length), lambda i: (i, 0))
    return pl.pallas_call(
        gate_kernel,
        grid=(channels // block,),
        in_specs=[
            pl.BlockSpec((block * LANES, LANES), lambda i: (i, 0)),
            line,
            line,
            pl.BlockSpec((block, LANES), lambda i: (i, 0)),
        ],
        out_specs=line,
        out_shape=jax.ShapeDtypeStruct((channels, length), BF16),
        name="gate",
    )(conv, signal, gate_values, skip)


def tables():
    first, third, mid = host_tables()
    first_hi, first_lo = halves_of(first)
    back_hi, back_lo = halves_of(first.T.copy())
    third_hi, third_lo = halves_of(third)
    undo_hi, undo_lo = halves_of(third.T.copy() / TOTAL)
    return dict(
        first=(first_hi, first_lo), back=(back_hi, back_lo), third=(third_hi, third_lo),
        undo=(undo_hi, undo_lo), mid=mid,
    )


def transform_taps(taps, tab, twiddle):
    return pl.pallas_call(
        taps_kernel,
        out_shape=jax.ShapeDtypeStruct((MIDS, ROWS, 2 * LANES), F32),
        scratch_shapes=[pltpu.VMEM((MIDS, ROWS, LANES), F32)] * 2,
        name="taps",
    )(taps, *tab["first"], *tab["third"], tab["mid"], *twiddle)


def convolve(values, spectrum, tab, twiddle):
    return pl.pallas_call(
        signal_kernel,
        out_shape=jax.ShapeDtypeStruct(values.shape, F32),
        scratch_shapes=[pltpu.VMEM((MIDS, ROWS, LANES), F32)] * 2,
        name="convolve",
    )(values, spectrum, *tab["first"], *tab["back"], *tab["third"], *tab["undo"], tab["mid"], *twiddle)


def shards(signal, filter_taps, gate_values, skip_gain):
    channels, length = signal.shape
    blocks = lax.axis_size("ctx")
    shape = (blocks, MIDS, ROWS // blocks, LANES)
    tab = {k: jax.tree.map(jnp.asarray, v) for k, v in tables().items()}

    def exchange(values):
        return lax.all_to_all(values.reshape(shape), "ctx", split_axis=0, concat_axis=0, tiled=True)

    taps = exchange(pack(filter_taps))
    values = exchange(pack(signal))
    twiddle = row_twiddle()
    spectrum = transform_taps(taps, tab, twiddle)
    conv = convolve(values, spectrum, tab, twiddle)
    back = exchange(conv).reshape(channels * LANES, LANES)
    return gate(back, signal, gate_values, skip_gain)


def solution(mesh):
    in_specs = (P("ch", "ctx"), P("ch", "ctx"), P("ch", "ctx"), P("ch"))
    out_specs = P("ch", "ctx")
    return jax.shard_map(shards, mesh=mesh, in_specs=in_specs, out_specs=out_specs, check_vma=False)
```

```python
import math

import jax
import jax.numpy as jnp
import numpy as np
from jax import lax
from jax.experimental import pallas as pl
from jax.experimental.pallas import tpu as pltpu
from jax.sharding import PartitionSpec as P

F32 = jnp.float32
BF16 = jnp.bfloat16
ROWS = 256
MIDS = 16
LANES = 128
TOTAL = ROWS * MIDS * LANES


def wave(product, period):
    angle = 2.0 * np.pi * (product % period) / period
    return np.cos(angle), np.sin(angle)


def halves_of(table):
    upper = table.astype(jnp.bfloat16)
    lower = (table - upper.astype(np.float64)).astype(jnp.bfloat16)
    return upper, lower


def host_tables():
    n1 = np.arange(ROWS, dtype=np.int64)
    k1 = np.arange(ROWS, dtype=np.int64)
    cos1, sin1 = wave((4 * k1[:, None] + 1) * n1[None, :], 4 * ROWS)
    first = np.concatenate([cos1, -sin1], axis=0)
    lane = np.arange(LANES, dtype=np.int64)
    cos3, sin3 = wave(lane[:, None] * lane[None, :], LANES)
    third = np.block([[cos3, -sin3], [sin3, cos3]])
    k2 = np.arange(MIDS, dtype=np.int64)
    cos2, sin2 = wave(k2[:, None] * lane[None, :], MIDS * LANES)
    mid = np.stack([cos2, -sin2]).astype(np.float32)
    cosp, sinp = wave((4 * k1[:, None] + 1) * lane[None, :], 4 * TOTAL)
    cose, sine = wave(np.broadcast_to((4 * k1[:, None] + 1) * LANES, (ROWS, LANES)), 4 * TOTAL)
    twist = np.stack([cosp, -sinp, cose, -sine]).astype(np.float32)
    return first, third, mid, twist


def split(values):
    upper = values.astype(BF16)
    return upper, (values - upper.astype(F32)).astype(BF16)


def dot(left, right):
    return jnp.dot(left, right, preferred_element_type=F32)


def times(a, b):
    return a[0] * b[0] - a[1] * b[1], a[0] * b[1] + a[1] * b[0]


def conj_times(a, b):
    return a[0] * b[0] + a[1] * b[1], a[1] * b[0] - a[0] * b[1]


def four_point(v, sign):
    s0 = (v[0][0] + v[2][0], v[0][1] + v[2][1])
    d0 = (v[0][0] - v[2][0], v[0][1] - v[2][1])
    s1 = (v[1][0] + v[3][0], v[1][1] + v[3][1])
    d1 = (v[1][0] - v[3][0], v[1][1] - v[3][1])
    r1 = (-sign * d1[1], sign * d1[0]) if sign > 0 else (d1[1], -d1[0])
    return [
        (s0[0] + s1[0], s0[1] + s1[1]),
        (d0[0] + r1[0], d0[1] + r1[1]),
        (s0[0] - s1[0], s0[1] - s1[1]),
        (d0[0] - r1[0], d0[1] - r1[1]),
    ]


def turn(v, step, sign):
    step = step % 16
    if step == 0:
        return v
    root = math.sqrt(0.5)
    if step == 2:
        if sign < 0:
            return ((v[0] + v[1]) * root, (v[1] - v[0]) * root)
        return ((v[0] - v[1]) * root, (v[1] + v[0]) * root)
    if step == 4:
        return (v[1], -v[0]) if sign < 0 else (-v[1], v[0])
    c, s = math.cos(2 * math.pi * step / 16), sign * math.sin(2 * math.pi * step / 16)
    return (v[0] * c - v[1] * s, v[0] * s + v[1] * c)


def sixteen_point(v, sign):
    columns = [four_point([v[4 * p + q] for p in range(4)], sign) for q in range(4)]
    out = [None] * 16
    for r in range(4):
        row = four_point([turn(columns[q][r], q * r, sign) for q in range(4)], sign)
        for s in range(4):
            out[r + 4 * s] = row[s]
    return out


NEAR = LANES // MIDS
BLOCK = 64
HBM = pl.BlockSpec(memory_space=pltpu.HBM)
ANY = pl.BlockSpec(memory_space=pl.ANY)


def tile_view(values):
    channels, length = values.shape
    return values.reshape(channels // 8, 8, length // LANES, LANES).transpose(0, 2, 1, 3)


def send_chunks(buf, out_ref, sems, group):
    copies = [
        pltpu.make_async_copy(buf.at[group, :, c, :], out_ref.at[8 * group + c], sems.at[8 * group + c])
        for c in range(8)
    ]
    for copy in copies:
        copy.start()
    return copies


def pack_taps_kernel(src_ref, out_ref, buf, in_sems, out_sems):
    groups = src_ref.shape[0]
    loads = [pltpu.make_async_copy(src_ref.at[g], buf.at[g], in_sems.at[g]) for g in range(groups)]
    for load in loads:
        load.start()
    sends = []
    for g in range(groups):
        loads[g].wait()
        sends += send_chunks(buf, out_ref, out_sems, g)
    for send in sends:
        send.wait()


def pack_taps(values):
    channels, length = values.shape
    view = tile_view(values)
    return pl.pallas_call(
        pack_taps_kernel,
        in_specs=[HBM],
        out_specs=HBM,
        out_shape=jax.ShapeDtypeStruct((channels, length // LANES, LANES), F32),
        scratch_shapes=[
            pltpu.VMEM(view.shape, F32),
            pltpu.SemaphoreType.DMA((channels // 8,)),
            pltpu.SemaphoreType.DMA((channels,)),
        ],
        name="pack_taps",
    )(view)


def pack_kernel(src_ref, out_ref):
    channels, length = src_ref.shape
    rows = length // LANES
    for group in range(channels // 8):
        for row in range(rows):
            value = src_ref[pl.ds(8 * group, 8), pl.ds(row * LANES, LANES)].astype(F32)
            out_ref[pl.ds(8 * group * rows + row, 8, stride=rows), :] = value


def pack(values):
    channels, length = values.shape
    block = 16
    rows = length // LANES
    return pl.pallas_call(
        pack_kernel,
        grid=(channels // block,),
        in_specs=[pl.BlockSpec((block, length), lambda i: (i, 0))],
        out_specs=pl.BlockSpec((block * rows, LANES), lambda i: (i, 0)),
        out_shape=jax.ShapeDtypeStruct((channels * rows, LANES), F32),
        name="pack",
    )(values)


def gate_kernel(conv_ref, signal_ref, gate_ref, skip_ref, out_ref, buf, out, sems, out_sems):
    groups, rows = buf.shape[:2]
    loads = [
        pltpu.make_async_copy(conv_ref.at[8 * g + c], buf.at[g, :, c, :], sems.at[8 * g + c])
        for g in range(groups)
        for c in range(8)
    ]
    for load in loads:
        load.start()
    stores = []
    for g in range(groups):
        lines = pl.ds(8 * g, 8)
        skip = skip_ref[lines, :]
        for c in range(8):
            loads[8 * g + c].wait()
        for row in range(rows):
            where = (lines, pl.ds(row * LANES, LANES))
            total = buf[g, row] + skip * signal_ref[where].astype(F32)
            out[where] = (gate_ref[where].astype(F32) * total).astype(BF16)
        if g % 2:
            pair = pl.ds(8 * g - 8, 16)
            stores.append(pltpu.make_async_copy(out.at[pair, :], out_ref.at[pair, :], out_sems.at[g // 2]))
            stores[-1].start()
    for store in stores:
        store.wait()


def gate(conv, signal, gate_values, skip):
    channels, length = signal.shape
    rows = length // LANES
    vmem = pl.BlockSpec(memory_space=pltpu.VMEM)
    return pl.pallas_call(
        gate_kernel,
        in_specs=[ANY, vmem, vmem, vmem],
        out_specs=HBM,
        out_shape=jax.ShapeDtypeStruct((channels, length), BF16),
        scratch_shapes=[
            pltpu.VMEM((channels // 8, rows, 8, LANES), F32),
            pltpu.VMEM((channels, length), BF16),
            pltpu.SemaphoreType.DMA((channels,)),
            pltpu.SemaphoreType.DMA((channels // 16,)),
        ],
        compiler_params=pltpu.CompilerParams(vmem_limit_bytes=16 << 20),
        name="gate",
    )(conv, signal, gate_values, skip)


def forward_rows(src, loads, first_hi, first_lo, twist, turn_re, turn_im, work_re, work_im, exact):
    turn_re[...] = twist[0]
    turn_im[...] = twist[1]

    def step(pair, carry):
        for side in range(2):
            loads(2 * pair + side).wait()
        values = jnp.concatenate([src[2 * pair].reshape(ROWS, LANES), src[2 * pair + 1].reshape(ROWS, LANES)], axis=1)
        if exact:
            upper = values.astype(BF16)
            out = dot(first_hi[...], upper) + dot(first_lo[...], upper)
        else:
            upper, lower = split(values)
            out = dot(first_hi[...], upper) + (dot(first_lo[...], upper) + dot(first_hi[...], lower))
        turned = (turn_re[...], turn_im[...])
        for side in range(2):
            lanes = slice(side * LANES, (side + 1) * LANES)
            re, im = times((out[:ROWS, lanes], out[ROWS:, lanes]), turned)
            work_re[2 * pair + side] = re
            work_im[2 * pair + side] = im
            turned = times(turned, (twist[2], twist[3]))
        turn_re[...] = turned[0]
        turn_im[...] = turned[1]
        return carry

    lax.fori_loop(0, MIDS // 2, step, 0)


def forward_mids(mid_ref, work_re, work_im, base, out_re, out_im, place):
    rows, to = pl.ds(base, 8), pl.ds(place, 8)
    out = sixteen_point([(work_re[m, rows], work_im[m, rows]) for m in range(MIDS)], -1)
    for k in range(MIDS):
        value = out[k]
        if k:
            value = times(value, (mid_ref[0, k : k + 1], mid_ref[1, k : k + 1]))
        out_re[k, to] = value[0]
        out_im[k, to] = value[1]


def inverse_mids(mid_ref, twist, work_re, work_im, place, out_re, out_im, base):
    rows, to = pl.ds(place, 8), pl.ds(base, 8)
    values = []
    for k in range(MIDS):
        value = (work_re[k, rows], work_im[k, rows])
        if k:
            value = conj_times(value, (mid_ref[0, k : k + 1], mid_ref[1, k : k + 1]))
        values.append(value)
    out = sixteen_point(values, 1)
    turned = (twist[0, to], twist[1, to])
    step = (twist[2, to], twist[3, to])
    for m in range(MIDS):
        re, im = conj_times(out[m], turned)
        out_re[m, to] = re
        out_im[m, to] = im
        if m + 1 < MIDS:
            turned = times(turned, step)


def lane_stage(values, third_hi, third_lo):
    upper, lower = split(values)
    rows = values.shape[0]
    both = dot(jnp.concatenate([upper, lower], axis=0), third_hi[...])
    return both[:rows] + (both[rows:] + dot(upper, third_lo[...]))


def column(src_ref, buf, sems):
    return lambda m: pltpu.make_async_copy(src_ref.at[:, :, m, :], buf.at[m], sems.at[m])


def taps_kernel(
    src_ref, first_hi, first_lo, third_hi, third_lo, mid_ref, twist, out_ref,
    src, turn_re, turn_im, work_re, work_im, sems,
):
    loads = column(src_ref, src, sems)
    for m in range(MIDS):
        loads(m).start()
    forward_rows(src, loads, first_hi, first_lo, twist, turn_re, turn_im, work_re, work_im, False)

    def mids(group, carry):
        base = pl.multiple_of(group * 8, 8)
        forward_mids(mid_ref, work_re, work_im, base, work_re, work_im, base)
        return carry

    lax.fori_loop(0, ROWS // 8, mids, 0)

    def step(k, carry):
        values = jnp.concatenate([work_re[k], work_im[k]], axis=1)
        out_ref[k] = lane_stage(values, third_hi, third_lo)
        return carry

    lax.fori_loop(0, MIDS, step, 0)


SMALL = ("first_hi", "first_lo", "back", "back_hi", "third_hi", "third_lo", "undo_hi", "undo_lo", "mid", "twist")


def convolve_kernel(src_ref, spec_ref, *refs):
    count = len(SMALL)
    tables, out_ref, scratch = refs[:count], refs[count], refs[count + 1 :]
    local, (src, spec, out, turn_re, turn_im, work_re, work_im, done_re, done_im) = scratch[:count], scratch[count : count + 9]
    blocks = [scratch[count + 9 + 4 * i : count + 13 + 4 * i] for i in range(2)]
    sems, table_sems, spec_sem, out_sems = scratch[count + 17 :]
    tab = dict(zip(SMALL, local))
    loads = column(src_ref, src, sems)
    table_loads = {
        name: pltpu.make_async_copy(tables[i], local[i], table_sems.at[i]) for i, name in enumerate(SMALL)
    }
    spec_load = pltpu.make_async_copy(spec_ref, spec, spec_sem)
    early = ("first_hi", "first_lo", "twist")
    for name in early:
        table_loads[name].start()
    for m in range(MIDS):
        loads(m).start()
    for name in SMALL:
        if name not in early:
            table_loads[name].start()
    spec_load.start()
    for name in early:
        table_loads[name].wait()
    forward_rows(src, loads, tab["first_hi"], tab["first_lo"], tab["twist"], turn_re, turn_im, work_re, work_im, True)
    for name in SMALL:
        if name not in early:
            table_loads[name].wait()
    spec_load.wait()
    mid, twist = tab["mid"], tab["twist"]

    def forward(j):
        for g in range(BLOCK // 8):
            forward_mids(mid, work_re, work_im, j * BLOCK + 8 * g, blocks[j % 2][0], blocks[j % 2][1], 8 * g)

    def backward(j):
        for g in range(BLOCK // 8):
            inverse_mids(mid, twist, blocks[j % 2][2], blocks[j % 2][3], 8 * g, done_re, done_im, j * BLOCK + 8 * g)

    def lanes(j):
        in_re, in_im, out_re, out_im = blocks[j % 2]
        rows = MIDS * BLOCK
        values = jnp.concatenate([in_re[...].reshape(rows, LANES), in_im[...].reshape(rows, LANES)], axis=1)
        seen = lane_stage(values, tab["third_hi"], tab["third_lo"])
        wave_h = spec[:, pl.ds(j * BLOCK, BLOCK), :].reshape(rows, 2 * LANES)
        prod = times((seen[:, :LANES], seen[:, LANES:]), (wave_h[:, :LANES], wave_h[:, LANES:]))
        back = lane_stage(jnp.concatenate(prod, axis=1), tab["undo_hi"], tab["undo_lo"])
        out_re[...] = back[:, :LANES].reshape(MIDS, BLOCK, LANES)
        out_im[...] = back[:, LANES:].reshape(MIDS, BLOCK, LANES)

    steps = ROWS // BLOCK
    forward(0)
    for j in range(steps):
        lanes(j)
        if j + 1 < steps:
            forward(j + 1)
        if j:
            backward(j - 1)
    backward(steps - 1)

    def store(m):
        return pltpu.make_async_copy(out.at[m], out_ref.at[:, :, m, :], out_sems.at[m])

    def last(pair, carry):
        values = jnp.concatenate(
            [
                jnp.concatenate([done_re[2 * pair], done_im[2 * pair]], axis=0),
                jnp.concatenate([done_re[2 * pair + 1], done_im[2 * pair + 1]], axis=0),
            ],
            axis=1,
        )
        upper, lower = split(values)
        both = dot(tab["back"][...], upper)
        result = both[:ROWS] + (both[ROWS:] + dot(tab["back_hi"][...], lower))
        for side in range(2):
            out[2 * pair + side] = result[:, side * LANES : (side + 1) * LANES].reshape(out.shape[1:])
            store(2 * pair + side).start()
        return carry

    lax.fori_loop(0, MIDS // 2, last, 0)
    for m in range(MIDS):
        store(m).wait()


def tables():
    first, third, mid, twist = host_tables()
    first_hi, first_lo = halves_of(first)
    back_hi, back_lo = halves_of(first.T.copy())
    third_hi, third_lo = halves_of(third)
    undo_hi, undo_lo = halves_of(third.T.copy() / TOTAL)
    return dict(
        first_hi=first_hi, first_lo=first_lo, back=np.concatenate([back_hi, back_lo], axis=0), back_hi=back_hi,
        third_hi=third_hi, third_lo=third_lo, undo_hi=undo_hi, undo_lo=undo_lo, mid=mid, twist=twist,
    )


def column_scratch(blocks):
    return pltpu.VMEM((MIDS, blocks, ROWS // blocks, LANES), F32)


def transform_taps(taps, tab):
    names = ("first_hi", "first_lo", "third_hi", "third_lo", "mid", "twist")
    vmem = pl.BlockSpec(memory_space=pltpu.VMEM)
    return pl.pallas_call(
        taps_kernel,
        in_specs=[vmem] + [vmem] * len(names),
        out_shape=jax.ShapeDtypeStruct((MIDS, ROWS, 2 * LANES), F32),
        scratch_shapes=[column_scratch(taps.shape[0])]
        + [pltpu.VMEM((ROWS, LANES), F32)] * 2
        + [pltpu.VMEM((MIDS, ROWS, LANES), F32)] * 2
        + [pltpu.SemaphoreType.DMA((MIDS,))],
        compiler_params=pltpu.CompilerParams(vmem_limit_bytes=52 << 20),
        name="taps",
    )(taps, *(tab[n] for n in names))


def convolve(values, spectrum, tab):
    small = [tab[n] for n in SMALL]
    column_buf = column_scratch(values.shape[0])
    whole = pltpu.VMEM((MIDS, ROWS, LANES), F32)
    part = pltpu.VMEM((MIDS, BLOCK, LANES), F32)
    return pl.pallas_call(
        convolve_kernel,
        in_specs=[ANY] + [HBM] * (1 + len(small)),
        out_specs=HBM,
        out_shape=jax.ShapeDtypeStruct(values.shape, F32),
        scratch_shapes=[pltpu.VMEM(t.shape, t.dtype) for t in small]
        + [column_buf, pltpu.VMEM(spectrum.shape, F32), column_buf]
        + [pltpu.VMEM((ROWS, LANES), F32)] * 2
        + [whole] * 4
        + [part] * 8
        + [
            pltpu.SemaphoreType.DMA((MIDS,)),
            pltpu.SemaphoreType.DMA((len(small),)),
            pltpu.SemaphoreType.DMA(()),
            pltpu.SemaphoreType.DMA((MIDS,)),
        ],
        compiler_params=pltpu.CompilerParams(vmem_limit_bytes=58 << 20),
        name="convolve",
    )(values, spectrum, *small)


def shards(signal, filter_taps, gate_values, skip_gain):
    channels, length = signal.shape
    blocks = lax.axis_size("ctx")
    shape = (blocks, ROWS // blocks, MIDS, LANES)
    tab = {k: jnp.asarray(v) for k, v in tables().items()}

    def exchange(values):
        return lax.all_to_all(values.reshape(shape), "ctx", split_axis=0, concat_axis=0, tiled=True)

    taps = pltpu.with_memory_space_constraint(exchange(pack_taps(filter_taps)), pltpu.VMEM)
    skip = jnp.broadcast_to(skip_gain[:, None], (channels, LANES))
    packed, skip = lax.optimization_barrier((pack(signal), skip))
    values = exchange(packed)
    spectrum = transform_taps(taps, tab)
    conv = convolve(values, spectrum, tab)
    back = exchange(conv).reshape(channels, length // LANES, LANES)
    return gate(back, signal, gate_values, skip)


def solution(mesh):
    in_specs = (P("ch", "ctx"), P("ch", "ctx"), P("ch", "ctx"), P("ch"))
    out_specs = P("ch", "ctx")
    return jax.shard_map(shards, mesh=mesh, in_specs=in_specs, out_specs=out_specs, check_vma=False)
```

```python
import math

import jax
import jax.numpy as jnp
import numpy as np
from jax import lax
from jax.experimental import pallas as pl
from jax.experimental.pallas import tpu as pltpu
from jax.sharding import PartitionSpec as P

F32 = jnp.float32
BF16 = jnp.bfloat16
ROWS = 256
MIDS = 16
LANES = 128
TOTAL = ROWS * MIDS * LANES


def wave(product, period):
    angle = 2.0 * np.pi * (product % period) / period
    return np.cos(angle), np.sin(angle)


def halves_of(table):
    upper = table.astype(jnp.bfloat16)
    lower = (table - upper.astype(np.float64)).astype(jnp.bfloat16)
    return upper, lower


def host_tables():
    n1 = np.arange(ROWS, dtype=np.int64)
    k1 = np.arange(ROWS, dtype=np.int64)
    cos1, sin1 = wave((4 * k1[:, None] + 1) * n1[None, :], 4 * ROWS)
    first = np.concatenate([cos1, -sin1], axis=0)
    lane = np.arange(LANES, dtype=np.int64)
    cos3, sin3 = wave(lane[:, None] * lane[None, :], LANES)
    third = np.block([[cos3, -sin3], [sin3, cos3]])
    k2 = np.arange(MIDS, dtype=np.int64)
    cos2, sin2 = wave(k2[:, None] * lane[None, :], MIDS * LANES)
    mid = np.stack([cos2, -sin2]).astype(np.float32)
    cosp, sinp = wave((4 * k1[:, None] + 1) * lane[None, :], 4 * TOTAL)
    cose, sine = wave(np.broadcast_to((4 * k1[:, None] + 1) * LANES, (ROWS, LANES)), 4 * TOTAL)
    twist = np.stack([cosp, -sinp, cose, -sine]).astype(np.float32)
    return first, third, mid, twist


def split(values):
    upper = values.astype(BF16)
    return upper, (values - upper.astype(F32)).astype(BF16)


def dot(left, right):
    return jnp.dot(left, right, preferred_element_type=F32)


def times(a, b):
    return a[0] * b[0] - a[1] * b[1], a[0] * b[1] + a[1] * b[0]


def conj_times(a, b):
    return a[0] * b[0] + a[1] * b[1], a[1] * b[0] - a[0] * b[1]


def four_point(v, sign):
    s0 = (v[0][0] + v[2][0], v[0][1] + v[2][1])
    d0 = (v[0][0] - v[2][0], v[0][1] - v[2][1])
    s1 = (v[1][0] + v[3][0], v[1][1] + v[3][1])
    d1 = (v[1][0] - v[3][0], v[1][1] - v[3][1])
    r1 = (-sign * d1[1], sign * d1[0]) if sign > 0 else (d1[1], -d1[0])
    return [
        (s0[0] + s1[0], s0[1] + s1[1]),
        (d0[0] + r1[0], d0[1] + r1[1]),
        (s0[0] - s1[0], s0[1] - s1[1]),
        (d0[0] - r1[0], d0[1] - r1[1]),
    ]


def turn(v, step, sign):
    step = step % 16
    if step == 0:
        return v
    root = math.sqrt(0.5)
    if step == 2:
        if sign < 0:
            return ((v[0] + v[1]) * root, (v[1] - v[0]) * root)
        return ((v[0] - v[1]) * root, (v[1] + v[0]) * root)
    if step == 4:
        return (v[1], -v[0]) if sign < 0 else (-v[1], v[0])
    c, s = math.cos(2 * math.pi * step / 16), sign * math.sin(2 * math.pi * step / 16)
    return (v[0] * c - v[1] * s, v[0] * s + v[1] * c)


def sixteen_point(v, sign):
    columns = [four_point([v[4 * p + q] for p in range(4)], sign) for q in range(4)]
    out = [None] * 16
    for r in range(4):
        row = four_point([turn(columns[q][r], q * r, sign) for q in range(4)], sign)
        for s in range(4):
            out[r + 4 * s] = row[s]
    return out


NEAR = LANES // MIDS
STAGGER_NS = 15000
BLOCK = 64
HBM = pl.BlockSpec(memory_space=pltpu.HBM)
ANY = pl.BlockSpec(memory_space=pl.ANY)


def tile_view(values):
    channels, length = values.shape
    return values.reshape(channels // 8, 8, length // LANES, LANES).transpose(0, 2, 1, 3)


def send_chunks(buf, out_ref, sems, group):
    copies = [
        pltpu.make_async_copy(buf.at[group, :, c, :], out_ref.at[8 * group + c], sems.at[8 * group + c])
        for c in range(8)
    ]
    for copy in copies:
        copy.start()
    return copies


def pack_taps_kernel(late_ref, src_ref, out_ref, buf, in_sems, out_sems):
    groups = src_ref.shape[0]

    @pl.when(late_ref[0] == 1)
    def _():
        pl.delay(STAGGER_NS)

    loads = [pltpu.make_async_copy(src_ref.at[g], buf.at[g], in_sems.at[g]) for g in range(groups)]
    for load in loads:
        load.start()
    sends = []
    for g in range(groups):
        loads[g].wait()
        sends += send_chunks(buf, out_ref, out_sems, g)
    for send in sends:
        send.wait()


def pack_taps(values, late):
    channels, length = values.shape
    view = tile_view(values)
    return pl.pallas_call(
        pack_taps_kernel,
        in_specs=[pl.BlockSpec(memory_space=pltpu.SMEM), HBM],
        out_specs=HBM,
        out_shape=jax.ShapeDtypeStruct((channels, length // LANES, LANES), F32),
        scratch_shapes=[
            pltpu.VMEM(view.shape, F32),
            pltpu.SemaphoreType.DMA((channels // 8,)),
            pltpu.SemaphoreType.DMA((channels,)),
        ],
        name="pack_taps",
    )(late, view)


def pack_kernel(src_ref, out_ref):
    channels, length = src_ref.shape
    rows = length // LANES
    for group in range(channels // 8):
        for row in range(rows):
            value = src_ref[pl.ds(8 * group, 8), pl.ds(row * LANES, LANES)].astype(F32)
            out_ref[pl.ds(8 * group * rows + row, 8, stride=rows), :] = value


def pack(values):
    channels, length = values.shape
    block = 16
    rows = length // LANES
    return pl.pallas_call(
        pack_kernel,
        grid=(channels // block,),
        in_specs=[pl.BlockSpec((block, length), lambda i: (i, 0))],
        out_specs=pl.BlockSpec((block * rows, LANES), lambda i: (i, 0)),
        out_shape=jax.ShapeDtypeStruct((channels * rows, LANES), F32),
        name="pack",
    )(values)


def gate_kernel(conv_ref, signal_ref, gate_ref, skip_ref, out_ref, buf, out, sems, out_sems):
    groups, rows = buf.shape[:2]
    loads = [
        pltpu.make_async_copy(conv_ref.at[8 * g + c], buf.at[g, :, c, :], sems.at[8 * g + c])
        for g in range(groups)
        for c in range(8)
    ]
    for load in loads:
        load.start()
    stores = []
    for g in range(groups):
        lines = pl.ds(8 * g, 8)
        skip = skip_ref[lines, :]
        for c in range(8):
            loads[8 * g + c].wait()
        for row in range(rows):
            where = (lines, pl.ds(row * LANES, LANES))
            total = buf[g, row] + skip * signal_ref[where].astype(F32)
            out[where] = (gate_ref[where].astype(F32) * total).astype(BF16)
        if g % 2:
            pair = pl.ds(8 * g - 8, 16)
            stores.append(pltpu.make_async_copy(out.at[pair, :], out_ref.at[pair, :], out_sems.at[g // 2]))
            stores[-1].start()
    for store in stores:
        store.wait()


def gate(conv, signal, gate_values, skip):
    channels, length = signal.shape
    rows = length // LANES
    vmem = pl.BlockSpec(memory_space=pltpu.VMEM)
    return pl.pallas_call(
        gate_kernel,
        in_specs=[ANY, vmem, vmem, vmem],
        out_specs=HBM,
        out_shape=jax.ShapeDtypeStruct((channels, length), BF16),
        scratch_shapes=[
            pltpu.VMEM((channels // 8, rows, 8, LANES), F32),
            pltpu.VMEM((channels, length), BF16),
            pltpu.SemaphoreType.DMA((channels,)),
            pltpu.SemaphoreType.DMA((channels // 16,)),
        ],
        compiler_params=pltpu.CompilerParams(vmem_limit_bytes=16 << 20),
        name="gate",
    )(conv, signal, gate_values, skip)


def forward_rows(src, loads, first_hi, first_lo, twist, turn_re, turn_im, work_re, work_im, exact):
    turn_re[...] = twist[0]
    turn_im[...] = twist[1]

    def step(pair, carry):
        for side in range(2):
            loads(2 * pair + side).wait()
        values = jnp.concatenate([src[2 * pair].reshape(ROWS, LANES), src[2 * pair + 1].reshape(ROWS, LANES)], axis=1)
        if exact:
            upper = values.astype(BF16)
            out = dot(first_hi[...], upper) + dot(first_lo[...], upper)
        else:
            upper, lower = split(values)
            out = dot(first_hi[...], upper) + (dot(first_lo[...], upper) + dot(first_hi[...], lower))
        turned = (turn_re[...], turn_im[...])
        for side in range(2):
            lanes = slice(side * LANES, (side + 1) * LANES)
            re, im = times((out[:ROWS, lanes], out[ROWS:, lanes]), turned)
            work_re[2 * pair + side] = re
            work_im[2 * pair + side] = im
            turned = times(turned, (twist[2], twist[3]))
        turn_re[...] = turned[0]
        turn_im[...] = turned[1]
        return carry

    lax.fori_loop(0, MIDS // 2, step, 0)


def forward_mids(mid_ref, work_re, work_im, base, out_re, out_im, place):
    rows, to = pl.ds(base, 8), pl.ds(place, 8)
    out = sixteen_point([(work_re[m, rows], work_im[m, rows]) for m in range(MIDS)], -1)
    for k in range(MIDS):
        value = out[k]
        if k:
            value = times(value, (mid_ref[0, k : k + 1], mid_ref[1, k : k + 1]))
        out_re[k, to] = value[0]
        out_im[k, to] = value[1]


def inverse_mids(mid_ref, twist, work_re, work_im, place, out_re, out_im, base):
    rows, to = pl.ds(place, 8), pl.ds(base, 8)
    values = []
    for k in range(MIDS):
        value = (work_re[k, rows], work_im[k, rows])
        if k:
            value = conj_times(value, (mid_ref[0, k : k + 1], mid_ref[1, k : k + 1]))
        values.append(value)
    out = sixteen_point(values, 1)
    turned = (twist[0, to], twist[1, to])
    step = (twist[2, to], twist[3, to])
    for m in range(MIDS):
        re, im = conj_times(out[m], turned)
        out_re[m, to] = re
        out_im[m, to] = im
        if m + 1 < MIDS:
            turned = times(turned, step)


def lane_stage(values, third_hi, third_lo):
    upper, lower = split(values)
    rows = values.shape[0]
    both = dot(jnp.concatenate([upper, lower], axis=0), third_hi[...])
    return both[:rows] + (both[rows:] + dot(upper, third_lo[...]))


def column(src_ref, buf, sems):
    return lambda m: pltpu.make_async_copy(src_ref.at[:, :, m, :], buf.at[m], sems.at[m])


def taps_kernel(
    src_ref, first_hi, first_lo, third_hi, third_lo, mid_ref, twist, out_ref,
    src, turn_re, turn_im, work_re, work_im, sems,
):
    loads = column(src_ref, src, sems)
    for m in range(MIDS):
        loads(m).start()
    forward_rows(src, loads, first_hi, first_lo, twist, turn_re, turn_im, work_re, work_im, False)

    def mids(group, carry):
        base = pl.multiple_of(group * 8, 8)
        forward_mids(mid_ref, work_re, work_im, base, work_re, work_im, base)
        return carry

    lax.fori_loop(0, ROWS // 8, mids, 0)

    def step(k, carry):
        values = jnp.concatenate([work_re[k], work_im[k]], axis=1)
        out_ref[k] = lane_stage(values, third_hi, third_lo)
        return carry

    lax.fori_loop(0, MIDS, step, 0)


SMALL = ("first_hi", "first_lo", "back", "back_hi", "third_hi", "third_lo", "undo_hi", "undo_lo", "mid", "twist")


def convolve_kernel(src_ref, spec_ref, *refs):
    count = len(SMALL)
    tables, out_ref, scratch = refs[:count], refs[count], refs[count + 1 :]
    local, (src, spec, out, turn_re, turn_im, work_re, work_im, done_re, done_im) = scratch[:count], scratch[count : count + 9]
    blocks = [scratch[count + 9 + 4 * i : count + 13 + 4 * i] for i in range(2)]
    sems, table_sems, spec_sem, out_sems = scratch[count + 17 :]
    tab = dict(zip(SMALL, local))
    loads = column(src_ref, src, sems)
    table_loads = {
        name: pltpu.make_async_copy(tables[i], local[i], table_sems.at[i]) for i, name in enumerate(SMALL)
    }
    spec_load = pltpu.make_async_copy(spec_ref, spec, spec_sem)
    early = ("first_hi", "first_lo", "twist")
    for name in early:
        table_loads[name].start()
    for m in range(MIDS):
        loads(m).start()
    for name in SMALL:
        if name not in early:
            table_loads[name].start()
    spec_load.start()
    for name in early:
        table_loads[name].wait()
    forward_rows(src, loads, tab["first_hi"], tab["first_lo"], tab["twist"], turn_re, turn_im, work_re, work_im, True)
    for name in SMALL:
        if name not in early:
            table_loads[name].wait()
    spec_load.wait()
    mid, twist = tab["mid"], tab["twist"]

    def forward(j):
        for g in range(BLOCK // 8):
            forward_mids(mid, work_re, work_im, j * BLOCK + 8 * g, blocks[j % 2][0], blocks[j % 2][1], 8 * g)

    def backward(j):
        for g in range(BLOCK // 8):
            inverse_mids(mid, twist, blocks[j % 2][2], blocks[j % 2][3], 8 * g, done_re, done_im, j * BLOCK + 8 * g)

    def lanes(j):
        in_re, in_im, out_re, out_im = blocks[j % 2]
        rows = MIDS * BLOCK
        values = jnp.concatenate([in_re[...].reshape(rows, LANES), in_im[...].reshape(rows, LANES)], axis=1)
        seen = lane_stage(values, tab["third_hi"], tab["third_lo"])
        wave_h = spec[:, pl.ds(j * BLOCK, BLOCK), :].reshape(rows, 2 * LANES)
        prod = times((seen[:, :LANES], seen[:, LANES:]), (wave_h[:, :LANES], wave_h[:, LANES:]))
        back = lane_stage(jnp.concatenate(prod, axis=1), tab["undo_hi"], tab["undo_lo"])
        out_re[...] = back[:, :LANES].reshape(MIDS, BLOCK, LANES)
        out_im[...] = back[:, LANES:].reshape(MIDS, BLOCK, LANES)

    steps = ROWS // BLOCK
    forward(0)
    for j in range(steps):
        lanes(j)
        if j + 1 < steps:
            forward(j + 1)
        if j:
            backward(j - 1)
    backward(steps - 1)

    def store(m):
        return pltpu.make_async_copy(out.at[m], out_ref.at[:, :, m, :], out_sems.at[m])

    def last(pair, carry):
        values = jnp.concatenate(
            [
                jnp.concatenate([done_re[2 * pair], done_im[2 * pair]], axis=0),
                jnp.concatenate([done_re[2 * pair + 1], done_im[2 * pair + 1]], axis=0),
            ],
            axis=1,
        )
        upper, lower = split(values)
        both = dot(tab["back"][...], upper)
        result = both[:ROWS] + (both[ROWS:] + dot(tab["back_hi"][...], lower))
        for side in range(2):
            out[2 * pair + side] = result[:, side * LANES : (side + 1) * LANES].reshape(out.shape[1:])
            store(2 * pair + side).start()
        return carry

    lax.fori_loop(0, MIDS // 2, last, 0)
    for m in range(MIDS):
        store(m).wait()


def tables():
    first, third, mid, twist = host_tables()
    first_hi, first_lo = halves_of(first)
    back_hi, back_lo = halves_of(first.T.copy())
    third_hi, third_lo = halves_of(third)
    undo_hi, undo_lo = halves_of(third.T.copy() / TOTAL)
    return dict(
        first_hi=first_hi, first_lo=first_lo, back=np.concatenate([back_hi, back_lo], axis=0), back_hi=back_hi,
        third_hi=third_hi, third_lo=third_lo, undo_hi=undo_hi, undo_lo=undo_lo, mid=mid, twist=twist,
    )


def column_scratch(blocks):
    return pltpu.VMEM((MIDS, blocks, ROWS // blocks, LANES), F32)


def transform_taps(taps, tab):
    names = ("first_hi", "first_lo", "third_hi", "third_lo", "mid", "twist")
    vmem = pl.BlockSpec(memory_space=pltpu.VMEM)
    return pl.pallas_call(
        taps_kernel,
        in_specs=[vmem] + [vmem] * len(names),
        out_shape=jax.ShapeDtypeStruct((MIDS, ROWS, 2 * LANES), F32),
        scratch_shapes=[column_scratch(taps.shape[0])]
        + [pltpu.VMEM((ROWS, LANES), F32)] * 2
        + [pltpu.VMEM((MIDS, ROWS, LANES), F32)] * 2
        + [pltpu.SemaphoreType.DMA((MIDS,))],
        compiler_params=pltpu.CompilerParams(vmem_limit_bytes=52 << 20),
        name="taps",
    )(taps, *(tab[n] for n in names))


def convolve(values, spectrum, tab):
    small = [tab[n] for n in SMALL]
    column_buf = column_scratch(values.shape[0])
    whole = pltpu.VMEM((MIDS, ROWS, LANES), F32)
    part = pltpu.VMEM((MIDS, BLOCK, LANES), F32)
    return pl.pallas_call(
        convolve_kernel,
        in_specs=[ANY] + [HBM] * (1 + len(small)),
        out_specs=HBM,
        out_shape=jax.ShapeDtypeStruct(values.shape, F32),
        scratch_shapes=[pltpu.VMEM(t.shape, t.dtype) for t in small]
        + [column_buf, pltpu.VMEM(spectrum.shape, F32), column_buf]
        + [pltpu.VMEM((ROWS, LANES), F32)] * 2
        + [whole] * 4
        + [part] * 8
        + [
            pltpu.SemaphoreType.DMA((MIDS,)),
            pltpu.SemaphoreType.DMA((len(small),)),
            pltpu.SemaphoreType.DMA(()),
            pltpu.SemaphoreType.DMA((MIDS,)),
        ],
        compiler_params=pltpu.CompilerParams(vmem_limit_bytes=58 << 20),
        name="convolve",
    )(values, spectrum, *small)


def shards(signal, filter_taps, gate_values, skip_gain):
    channels, length = signal.shape
    blocks = lax.axis_size("ctx")
    shape = (blocks, ROWS // blocks, MIDS, LANES)
    tab = {k: jnp.asarray(v) for k, v in tables().items()}

    late = (lax.axis_index("ch") % 2).astype(jnp.int32).reshape(1)

    def exchange(values):
        return lax.all_to_all(values.reshape(shape), "ctx", split_axis=0, concat_axis=0, tiled=True)

    taps = pltpu.with_memory_space_constraint(exchange(pack_taps(filter_taps, late)), pltpu.VMEM)
    skip = jnp.broadcast_to(skip_gain[:, None], (channels, LANES))
    packed, skip = lax.optimization_barrier((pack(signal), skip))
    values = exchange(packed)
    spectrum = transform_taps(taps, tab)
    conv = convolve(values, spectrum, tab)
    back = exchange(conv).reshape(channels, length // LANES, LANES)
    return gate(back, signal, gate_values, skip)


def solution(mesh):
    in_specs = (P("ch", "ctx"), P("ch", "ctx"), P("ch", "ctx"), P("ch"))
    out_specs = P("ch", "ctx")
    return jax.shard_map(shards, mesh=mesh, in_specs=in_specs, out_specs=out_specs, check_vma=False)
```

```python
import math

import jax
import jax.numpy as jnp
import numpy as np
from jax import lax
from jax.experimental import pallas as pl
from jax.experimental.pallas import tpu as pltpu
from jax.sharding import PartitionSpec as P

F32 = jnp.float32
BF16 = jnp.bfloat16
ROWS = 256
MIDS = 16
LANES = 128
TOTAL = ROWS * MIDS * LANES


def wave(product, period):
    angle = 2.0 * np.pi * (product % period) / period
    return np.cos(angle), np.sin(angle)


def halves_of(table):
    upper = table.astype(jnp.bfloat16)
    lower = (table - upper.astype(np.float64)).astype(jnp.bfloat16)
    return upper, lower


def host_tables():
    n1 = np.arange(ROWS, dtype=np.int64)
    k1 = np.arange(ROWS, dtype=np.int64)
    cos1, sin1 = wave((4 * k1[:, None] + 1) * n1[None, :], 4 * ROWS)
    first = np.concatenate([cos1, -sin1], axis=0)
    lane = np.arange(LANES, dtype=np.int64)
    cos3, sin3 = wave(lane[:, None] * lane[None, :], LANES)
    third = np.block([[cos3, -sin3], [sin3, cos3]])
    k2 = np.arange(MIDS, dtype=np.int64)
    cos2, sin2 = wave(k2[:, None] * lane[None, :], MIDS * LANES)
    mid = np.stack([cos2, -sin2]).astype(np.float32)
    cosp, sinp = wave((4 * k1[:, None] + 1) * lane[None, :], 4 * TOTAL)
    cose, sine = wave(np.broadcast_to((4 * k1[:, None] + 1) * LANES, (ROWS, LANES)), 4 * TOTAL)
    twist = np.stack([cosp, -sinp, cose, -sine]).astype(np.float32)
    return first, third, mid, twist


def split(values):
    upper = values.astype(BF16)
    return upper, (values - upper.astype(F32)).astype(BF16)


def dot(left, right):
    return jnp.dot(left, right, preferred_element_type=F32)


def times(a, b):
    return a[0] * b[0] - a[1] * b[1], a[0] * b[1] + a[1] * b[0]


def conj_times(a, b):
    return a[0] * b[0] + a[1] * b[1], a[1] * b[0] - a[0] * b[1]


def four_point(v, sign):
    s0 = (v[0][0] + v[2][0], v[0][1] + v[2][1])
    d0 = (v[0][0] - v[2][0], v[0][1] - v[2][1])
    s1 = (v[1][0] + v[3][0], v[1][1] + v[3][1])
    d1 = (v[1][0] - v[3][0], v[1][1] - v[3][1])
    r1 = (-sign * d1[1], sign * d1[0]) if sign > 0 else (d1[1], -d1[0])
    return [
        (s0[0] + s1[0], s0[1] + s1[1]),
        (d0[0] + r1[0], d0[1] + r1[1]),
        (s0[0] - s1[0], s0[1] - s1[1]),
        (d0[0] - r1[0], d0[1] - r1[1]),
    ]


def turn(v, step, sign):
    step = step % 16
    if step == 0:
        return v
    root = math.sqrt(0.5)
    if step == 2:
        if sign < 0:
            return ((v[0] + v[1]) * root, (v[1] - v[0]) * root)
        return ((v[0] - v[1]) * root, (v[1] + v[0]) * root)
    if step == 4:
        return (v[1], -v[0]) if sign < 0 else (-v[1], v[0])
    c, s = math.cos(2 * math.pi * step / 16), sign * math.sin(2 * math.pi * step / 16)
    return (v[0] * c - v[1] * s, v[0] * s + v[1] * c)


def sixteen_point(v, sign):
    columns = [four_point([v[4 * p + q] for p in range(4)], sign) for q in range(4)]
    out = [None] * 16
    for r in range(4):
        row = four_point([turn(columns[q][r], q * r, sign) for q in range(4)], sign)
        for s in range(4):
            out[r + 4 * s] = row[s]
    return out


NEAR = LANES // MIDS
STAGGER_NS = 15000
UNROLL = 16
BLOCK = 64
HBM = pl.BlockSpec(memory_space=pltpu.HBM)
ANY = pl.BlockSpec(memory_space=pl.ANY)


def tile_view(values):
    channels, length = values.shape
    return values.reshape(channels // 8, 8, length // LANES, LANES).transpose(0, 2, 1, 3)


def pack_taps_kernel(late_ref, src_ref, out_ref, buf, lines, in_sems, out_sems):
    groups, rows = src_ref.shape[:2]

    @pl.when(late_ref[0] == 1)
    def _():
        pl.delay(STAGGER_NS)

    loads = [pltpu.make_async_copy(src_ref.at[g], buf.at[g], in_sems.at[g]) for g in range(groups)]
    copied = range(groups // 2, groups)
    for g in copied:
        loads[g].start()
    for g in range(groups // 2):
        loads[g].start()
    sends = []
    for g in copied:
        loads[g].wait()
        for c in range(8):
            channel = 8 * g + c
            sends.append(pltpu.make_async_copy(buf.at[g, :, c, :], out_ref.at[channel], out_sems.at[channel]))
            sends[-1].start()
    for g in range(groups // 2):
        loads[g].wait()

        def spread(step, carry, g=g):
            for i in range(UNROLL):
                row = step * UNROLL + i
                lines[pl.ds(8 * g * rows + row, 8, stride=rows), :] = buf[g, row]
            return carry

        lax.fori_loop(0, rows // UNROLL, spread, 0)
        for c in range(8):
            channel = 8 * g + c
            sends.append(
                pltpu.make_async_copy(lines.at[pl.ds(channel * rows, rows), :], out_ref.at[channel], out_sems.at[channel])
            )
            sends[-1].start()
    for send in sends:
        send.wait()


def pack_taps(values, late):
    channels, length = values.shape
    view = tile_view(values)
    return pl.pallas_call(
        pack_taps_kernel,
        in_specs=[pl.BlockSpec(memory_space=pltpu.SMEM), HBM],
        out_specs=HBM,
        out_shape=jax.ShapeDtypeStruct((channels, length // LANES, LANES), F32),
        scratch_shapes=[
            pltpu.VMEM(view.shape, F32),
            pltpu.VMEM((channels // 2 * view.shape[1], LANES), F32),
            pltpu.SemaphoreType.DMA((channels // 8,)),
            pltpu.SemaphoreType.DMA((channels,)),
        ],
        name="pack_taps",
    )(late, view)


def pack_kernel(src_ref, out_ref):
    channels, length = src_ref.shape
    rows = length // LANES
    for group in range(channels // 8):

        def spread(step, carry, group=group):
            for i in range(UNROLL):
                row = step * UNROLL + i
                lanes = pl.ds(pl.multiple_of(row * LANES, LANES), LANES)
                value = src_ref[pl.ds(8 * group, 8), lanes].astype(F32)
                out_ref[pl.ds(8 * group * rows + row, 8, stride=rows), :] = value
            return carry

        lax.fori_loop(0, rows // UNROLL, spread, 0)


def pack(values):
    channels, length = values.shape
    block = 16
    rows = length // LANES
    return pl.pallas_call(
        pack_kernel,
        grid=(channels // block,),
        in_specs=[pl.BlockSpec((block, length), lambda i: (i, 0))],
        out_specs=pl.BlockSpec((block * rows, LANES), lambda i: (i, 0)),
        out_shape=jax.ShapeDtypeStruct((channels * rows, LANES), F32),
        name="pack",
    )(values)


def gate_kernel(conv_ref, signal_ref, gate_ref, skip_ref, out_ref, buf, out, sems, out_sems):
    groups = signal_ref.shape[0] // 8
    rows = signal_ref.shape[1] // LANES
    direct = groups - buf.shape[0]
    loads = {
        8 * g + c: pltpu.make_async_copy(
            conv_ref.at[pl.ds((8 * g + c) * rows, rows), :], buf.at[g - direct, :, c, :], sems.at[8 * (g - direct) + c]
        )
        for g in range(direct, groups)
        for c in range(8)
    }
    for load in loads.values():
        load.start()
    stores = []
    for g in range(groups):
        lines = pl.ds(8 * g, 8)
        skip = skip_ref[lines, :]
        if g >= direct:
            for c in range(8):
                loads[8 * g + c].wait()

        def some(step, carry, g=g, lines=lines, skip=skip):
            for i in range(UNROLL):
                row = step * UNROLL + i
                where = (lines, pl.ds(pl.multiple_of(row * LANES, LANES), LANES))
                conv = buf[g - direct, row] if g >= direct else conv_ref[pl.ds(8 * g * rows + row, 8, stride=rows), :]
                total = conv + skip * signal_ref[where].astype(F32)
                out[where] = (gate_ref[where].astype(F32) * total).astype(BF16)
            return carry

        lax.fori_loop(0, rows // UNROLL, some, 0)
        if g % 2:
            pair = pl.ds(8 * g - 8, 16)
            stores.append(pltpu.make_async_copy(out.at[pair, :], out_ref.at[pair, :], out_sems.at[g // 2]))
            stores[-1].start()
    for store in stores:
        store.wait()


def gate(conv, signal, gate_values, skip):
    channels, length = signal.shape
    rows = length // LANES
    vmem = pl.BlockSpec(memory_space=pltpu.VMEM)
    return pl.pallas_call(
        gate_kernel,
        in_specs=[vmem] * 4,
        out_specs=HBM,
        out_shape=jax.ShapeDtypeStruct((channels, length), BF16),
        scratch_shapes=[
            pltpu.VMEM((channels // 16, rows, 8, LANES), F32),
            pltpu.VMEM((channels, length), BF16),
            pltpu.SemaphoreType.DMA((channels // 2,)),
            pltpu.SemaphoreType.DMA((channels // 16,)),
        ],
        compiler_params=pltpu.CompilerParams(vmem_limit_bytes=16 << 20),
        name="gate",
    )(conv, signal, gate_values, skip)


def forward_rows(src, loads, first_hi, first_lo, twist, turn_re, turn_im, work_re, work_im, exact):
    turn_re[...] = twist[0]
    turn_im[...] = twist[1]

    def step(pair, carry):
        for side in range(2):
            loads(2 * pair + side).wait()
        values = jnp.concatenate([src[2 * pair].reshape(ROWS, LANES), src[2 * pair + 1].reshape(ROWS, LANES)], axis=1)
        if exact:
            upper = values.astype(BF16)
            out = dot(first_hi[...], upper) + dot(first_lo[...], upper)
        else:
            upper, lower = split(values)
            out = dot(first_hi[...], upper) + (dot(first_lo[...], upper) + dot(first_hi[...], lower))
        turned = (turn_re[...], turn_im[...])
        for side in range(2):
            lanes = slice(side * LANES, (side + 1) * LANES)
            re, im = times((out[:ROWS, lanes], out[ROWS:, lanes]), turned)
            work_re[2 * pair + side] = re
            work_im[2 * pair + side] = im
            turned = times(turned, (twist[2], twist[3]))
        turn_re[...] = turned[0]
        turn_im[...] = turned[1]
        return carry

    lax.fori_loop(0, MIDS // 2, step, 0)


def forward_mids(mid_ref, work_re, work_im, base, out_re, out_im, place):
    rows, to = pl.ds(base, 8), pl.ds(place, 8)
    out = sixteen_point([(work_re[m, rows], work_im[m, rows]) for m in range(MIDS)], -1)
    for k in range(MIDS):
        value = out[k]
        if k:
            value = times(value, (mid_ref[0, k : k + 1], mid_ref[1, k : k + 1]))
        out_re[k, to] = value[0]
        out_im[k, to] = value[1]


def inverse_mids(mid_ref, twist, work_re, work_im, place, out_re, out_im, base):
    rows, to = pl.ds(place, 8), pl.ds(base, 8)
    values = []
    for k in range(MIDS):
        value = (work_re[k, rows], work_im[k, rows])
        if k:
            value = conj_times(value, (mid_ref[0, k : k + 1], mid_ref[1, k : k + 1]))
        values.append(value)
    out = sixteen_point(values, 1)
    turned = (twist[0, to], twist[1, to])
    step = (twist[2, to], twist[3, to])
    for m in range(MIDS):
        re, im = conj_times(out[m], turned)
        out_re[m, to] = re
        out_im[m, to] = im
        if m + 1 < MIDS:
            turned = times(turned, step)


def lane_stage(values, third_hi, third_lo):
    upper, lower = split(values)
    rows = values.shape[0]
    both = dot(jnp.concatenate([upper, lower], axis=0), third_hi[...])
    return both[:rows] + (both[rows:] + dot(upper, third_lo[...]))


def column(src_ref, buf, sems):
    return lambda m: pltpu.make_async_copy(src_ref.at[:, :, m, :], buf.at[m], sems.at[m])


def taps_kernel(
    src_ref, first_hi, first_lo, third_hi, third_lo, mid_ref, twist, out_ref,
    src, turn_re, turn_im, work_re, work_im, sems,
):
    loads = column(src_ref, src, sems)
    for m in range(MIDS):
        loads(m).start()
    forward_rows(src, loads, first_hi, first_lo, twist, turn_re, turn_im, work_re, work_im, False)

    def mids(group, carry):
        base = pl.multiple_of(group * 8, 8)
        forward_mids(mid_ref, work_re, work_im, base, work_re, work_im, base)
        return carry

    lax.fori_loop(0, ROWS // 8, mids, 0)

    def step(j, carry):
        rows = pl.ds(pl.multiple_of(j * BLOCK, BLOCK), BLOCK)
        parts = [work[:, rows, :].reshape(MIDS * BLOCK, LANES) for work in (work_re, work_im)]
        seen = lane_stage(jnp.concatenate(parts, axis=1), third_hi, third_lo)
        out_ref[:, rows, :] = seen.reshape(MIDS, BLOCK, 2 * LANES)
        return carry

    lax.fori_loop(0, ROWS // BLOCK, step, 0)


SMALL = ("first_hi", "first_lo", "back", "third_hi", "third_lo", "undo_hi", "undo_lo", "mid", "twist")


def convolve_kernel(src_ref, spec_ref, *refs):
    count = len(SMALL)
    tables, out_ref, scratch = refs[:count], refs[count], refs[count + 1 :]
    local, (src, spec, out, turn_re, turn_im, work_re, work_im, done_re, done_im) = scratch[:count], scratch[count : count + 9]
    blocks = [scratch[count + 9 + 4 * i : count + 13 + 4 * i] for i in range(2)]
    sems, table_sems, spec_sem, out_sems = scratch[count + 17 :]
    tab = dict(zip(SMALL, local))
    loads = column(src_ref, src, sems)
    table_loads = {
        name: pltpu.make_async_copy(tables[i], local[i], table_sems.at[i]) for i, name in enumerate(SMALL)
    }
    spec_load = pltpu.make_async_copy(spec_ref, spec, spec_sem)
    early = ("first_hi", "first_lo", "twist")
    for name in early:
        table_loads[name].start()
    for m in range(MIDS):
        loads(m).start()
    for name in SMALL:
        if name not in early:
            table_loads[name].start()
    spec_load.start()
    for name in early:
        table_loads[name].wait()
    forward_rows(src, loads, tab["first_hi"], tab["first_lo"], tab["twist"], turn_re, turn_im, work_re, work_im, True)
    for name in SMALL:
        if name not in early:
            table_loads[name].wait()
    spec_load.wait()
    mid, twist = tab["mid"], tab["twist"]

    def forward(j):
        for g in range(BLOCK // 8):
            forward_mids(mid, work_re, work_im, j * BLOCK + 8 * g, blocks[j % 2][0], blocks[j % 2][1], 8 * g)

    def backward(j):
        for g in range(BLOCK // 8):
            inverse_mids(mid, twist, blocks[j % 2][2], blocks[j % 2][3], 8 * g, done_re, done_im, j * BLOCK + 8 * g)

    def lanes(j):
        in_re, in_im, out_re, out_im = blocks[j % 2]
        rows = MIDS * BLOCK
        values = jnp.concatenate([in_re[...].reshape(rows, LANES), in_im[...].reshape(rows, LANES)], axis=1)
        seen = lane_stage(values, tab["third_hi"], tab["third_lo"])
        wave_h = spec[:, pl.ds(j * BLOCK, BLOCK), :].reshape(rows, 2 * LANES)
        prod = times((seen[:, :LANES], seen[:, LANES:]), (wave_h[:, :LANES], wave_h[:, LANES:]))
        back = lane_stage(jnp.concatenate(prod, axis=1), tab["undo_hi"], tab["undo_lo"])
        out_re[...] = back[:, :LANES].reshape(MIDS, BLOCK, LANES)
        out_im[...] = back[:, LANES:].reshape(MIDS, BLOCK, LANES)

    steps = ROWS // BLOCK
    forward(0)
    for j in range(steps):
        lanes(j)
        if j + 1 < steps:
            forward(j + 1)
        if j:
            backward(j - 1)
    backward(steps - 1)

    def store(m):
        return pltpu.make_async_copy(out.at[m], out_ref.at[:, :, m, :], out_sems.at[m])

    def last(pair, carry):
        values = jnp.concatenate(
            [
                jnp.concatenate([done_re[2 * pair], done_im[2 * pair]], axis=0),
                jnp.concatenate([done_re[2 * pair + 1], done_im[2 * pair + 1]], axis=0),
            ],
            axis=1,
        )
        upper, lower = split(values)
        both = dot(tab["back"][...], upper)
        result = both[:ROWS] + (both[ROWS:] + dot(tab["back"][:ROWS], lower))
        for side in range(2):
            out[2 * pair + side] = result[:, side * LANES : (side + 1) * LANES].reshape(out.shape[1:])
            store(2 * pair + side).start()
        return carry

    lax.fori_loop(0, MIDS // 2, last, 0)
    for m in range(MIDS):
        store(m).wait()


def tables():
    first, third, mid, twist = host_tables()
    first_hi, first_lo = halves_of(first)
    back_hi, back_lo = halves_of(first.T.copy())
    third_hi, third_lo = halves_of(third)
    undo_hi, undo_lo = halves_of(third.T.copy() / TOTAL)
    return dict(
        first_hi=first_hi, first_lo=first_lo, back=np.concatenate([back_hi, back_lo], axis=0),
        third_hi=third_hi, third_lo=third_lo, undo_hi=undo_hi, undo_lo=undo_lo, mid=mid, twist=twist,
    )


def column_scratch(blocks):
    return pltpu.VMEM((MIDS, blocks, ROWS // blocks, LANES), F32)


def transform_taps(taps, tab):
    names = ("first_hi", "first_lo", "third_hi", "third_lo", "mid", "twist")
    vmem = pl.BlockSpec(memory_space=pltpu.VMEM)
    return pl.pallas_call(
        taps_kernel,
        in_specs=[vmem] + [vmem] * len(names),
        out_shape=jax.ShapeDtypeStruct((MIDS, ROWS, 2 * LANES), F32),
        scratch_shapes=[column_scratch(taps.shape[0])]
        + [pltpu.VMEM((ROWS, LANES), F32)] * 2
        + [pltpu.VMEM((MIDS, ROWS, LANES), F32)] * 2
        + [pltpu.SemaphoreType.DMA((MIDS,))],
        compiler_params=pltpu.CompilerParams(vmem_limit_bytes=52 << 20),
        name="taps",
    )(taps, *(tab[n] for n in names))


def convolve(values, spectrum, tab):
    small = [tab[n] for n in SMALL]
    column_buf = column_scratch(values.shape[0])
    whole = pltpu.VMEM((MIDS, ROWS, LANES), F32)
    part = pltpu.VMEM((MIDS, BLOCK, LANES), F32)
    return pl.pallas_call(
        convolve_kernel,
        in_specs=[ANY] + [HBM] * (1 + len(small)),
        out_specs=HBM,
        out_shape=jax.ShapeDtypeStruct(values.shape, F32),
        scratch_shapes=[pltpu.VMEM(t.shape, t.dtype) for t in small]
        + [column_buf, pltpu.VMEM(spectrum.shape, F32), column_buf]
        + [pltpu.VMEM((ROWS, LANES), F32)] * 2
        + [whole] * 4
        + [part] * 8
        + [
            pltpu.SemaphoreType.DMA((MIDS,)),
            pltpu.SemaphoreType.DMA((len(small),)),
            pltpu.SemaphoreType.DMA(()),
            pltpu.SemaphoreType.DMA((MIDS,)),
        ],
        compiler_params=pltpu.CompilerParams(vmem_limit_bytes=58 << 20),
        name="convolve",
    )(values, spectrum, *small)


def shards(signal, filter_taps, gate_values, skip_gain):
    channels, length = signal.shape
    blocks = lax.axis_size("ctx")
    shape = (blocks, ROWS // blocks, MIDS, LANES)
    tab = {k: jnp.asarray(v) for k, v in tables().items()}

    late = (lax.axis_index("ch") % 2).astype(jnp.int32).reshape(1)

    def exchange(values):
        return lax.all_to_all(values.reshape(shape), "ctx", split_axis=0, concat_axis=0, tiled=True)

    taps = pltpu.with_memory_space_constraint(exchange(pack_taps(filter_taps, late)), pltpu.VMEM)
    skip = jnp.broadcast_to(skip_gain[:, None], (channels, LANES))
    packed, skip = lax.optimization_barrier((pack(signal), skip))
    values = exchange(packed)
    spectrum = transform_taps(taps, tab)
    conv = convolve(values, spectrum, tab)
    back = pltpu.with_memory_space_constraint(exchange(conv).reshape(channels * (length // LANES), LANES), pltpu.VMEM)
    return gate(back, signal, gate_values, skip)


def solution(mesh):
    in_specs = (P("ch", "ctx"), P("ch", "ctx"), P("ch", "ctx"), P("ch"))
    out_specs = P("ch", "ctx")
    return jax.shard_map(shards, mesh=mesh, in_specs=in_specs, out_specs=out_specs, check_vma=False)
```

```python
import math

import jax
import jax.numpy as jnp
import numpy as np
from jax import lax
from jax.experimental import pallas as pl
from jax.experimental.pallas import tpu as pltpu
from jax.sharding import PartitionSpec as P

F32 = jnp.float32
BF16 = jnp.bfloat16
ROWS = 256
MIDS = 16
LANES = 128
TOTAL = ROWS * MIDS * LANES


def wave(product, period):
    angle = 2.0 * np.pi * (product % period) / period
    return np.cos(angle), np.sin(angle)


def halves_of(table):
    upper = table.astype(jnp.bfloat16)
    lower = (table - upper.astype(np.float64)).astype(jnp.bfloat16)
    return upper, lower


def host_tables():
    n1 = np.arange(ROWS, dtype=np.int64)
    k1 = np.arange(ROWS, dtype=np.int64)
    cos1, sin1 = wave((4 * k1[:, None] + 1) * n1[None, :], 4 * ROWS)
    first = np.concatenate([cos1, -sin1], axis=0)
    lane = np.arange(LANES, dtype=np.int64)
    cos3, sin3 = wave(lane[:, None] * lane[None, :], LANES)
    third = np.block([[cos3, -sin3], [sin3, cos3]])
    k2 = np.arange(MIDS, dtype=np.int64)
    cos2, sin2 = wave(k2[:, None] * lane[None, :], MIDS * LANES)
    mid = np.stack([cos2, -sin2]).astype(np.float32)
    cosp, sinp = wave((4 * k1[:, None] + 1) * lane[None, :], 4 * TOTAL)
    cose, sine = wave(np.broadcast_to((4 * k1[:, None] + 1) * LANES, (ROWS, LANES)), 4 * TOTAL)
    twist = np.stack([cosp, -sinp, cose, -sine]).astype(np.float32)
    return first, third, mid, twist


def split(values):
    upper = values.astype(BF16)
    return upper, (values - upper.astype(F32)).astype(BF16)


def dot(left, right):
    return jnp.dot(left, right, preferred_element_type=F32)


def times(a, b):
    return a[0] * b[0] - a[1] * b[1], a[0] * b[1] + a[1] * b[0]


def conj_times(a, b):
    return a[0] * b[0] + a[1] * b[1], a[1] * b[0] - a[0] * b[1]


def four_point(v, sign):
    s0 = (v[0][0] + v[2][0], v[0][1] + v[2][1])
    d0 = (v[0][0] - v[2][0], v[0][1] - v[2][1])
    s1 = (v[1][0] + v[3][0], v[1][1] + v[3][1])
    d1 = (v[1][0] - v[3][0], v[1][1] - v[3][1])
    r1 = (-sign * d1[1], sign * d1[0]) if sign > 0 else (d1[1], -d1[0])
    return [
        (s0[0] + s1[0], s0[1] + s1[1]),
        (d0[0] + r1[0], d0[1] + r1[1]),
        (s0[0] - s1[0], s0[1] - s1[1]),
        (d0[0] - r1[0], d0[1] - r1[1]),
    ]


def turn(v, step, sign):
    step = step % 16
    if step == 0:
        return v
    root = math.sqrt(0.5)
    if step == 2:
        if sign < 0:
            return ((v[0] + v[1]) * root, (v[1] - v[0]) * root)
        return ((v[0] - v[1]) * root, (v[1] + v[0]) * root)
    if step == 4:
        return (v[1], -v[0]) if sign < 0 else (-v[1], v[0])
    c, s = math.cos(2 * math.pi * step / 16), sign * math.sin(2 * math.pi * step / 16)
    return (v[0] * c - v[1] * s, v[0] * s + v[1] * c)


def sixteen_point(v, sign):
    columns = [four_point([v[4 * p + q] for p in range(4)], sign) for q in range(4)]
    out = [None] * 16
    for r in range(4):
        row = four_point([turn(columns[q][r], q * r, sign) for q in range(4)], sign)
        for s in range(4):
            out[r + 4 * s] = row[s]
    return out


NEAR = LANES // MIDS
STAGGER_NS = 15000
BLOCK = 64
HBM = pl.BlockSpec(memory_space=pltpu.HBM)
ANY = pl.BlockSpec(memory_space=pl.ANY)


def tile_view(values):
    channels, length = values.shape
    return values.reshape(channels // 8, 8, length // LANES, LANES).transpose(0, 2, 1, 3)


def swap_eight(tiles):
    row = lax.broadcasted_iota(jnp.int32, tiles[0].shape, 0)
    tiles = list(tiles)
    for bit in (4, 2, 1):
        odd = (row & bit) != 0
        for low in range(8):
            if low & bit:
                continue
            high = low | bit
            first, second = tiles[low], tiles[high]
            tiles[low] = jnp.where(odd, pltpu.roll(second, bit, 0), first)
            tiles[high] = jnp.where(odd, second, pltpu.roll(first, 8 - bit, 0))
    return tiles


def pack_taps_kernel(late_ref, src_ref, out_ref, buf, lines, in_sems, out_sems):
    groups, rows = src_ref.shape[:2]

    @pl.when(late_ref[0] == 1)
    def _():
        pl.delay(STAGGER_NS)

    loads = [pltpu.make_async_copy(src_ref.at[g], buf.at[g], in_sems.at[g]) for g in range(groups)]
    for load in loads:
        load.start()
    sends = []
    for g in range(groups):
        loads[g].wait()

        def spread(step, carry, g=g):
            for part in range(2):
                base = step * 16 + 8 * part
                tiles = swap_eight([buf[g, base + i] for i in range(8)])
                for c in range(8):
                    lines[8 * g + c, pl.ds(pl.multiple_of(base, 8), 8), :] = tiles[c]
            return carry

        lax.fori_loop(0, rows // 16, spread, 0)
        part = pl.ds(8 * g, 8)
        sends.append(pltpu.make_async_copy(lines.at[part], out_ref.at[part], out_sems.at[g]))
        sends[-1].start()
    for send in sends:
        send.wait()


def pack_taps(values, late):
    channels, length = values.shape
    view = tile_view(values)
    return pl.pallas_call(
        pack_taps_kernel,
        in_specs=[pl.BlockSpec(memory_space=pltpu.SMEM), HBM],
        out_specs=HBM,
        out_shape=jax.ShapeDtypeStruct((channels, length // LANES, LANES), F32),
        scratch_shapes=[
            pltpu.VMEM(view.shape, F32),
            pltpu.VMEM((channels, length // LANES, LANES), F32),
            pltpu.SemaphoreType.DMA((channels // 8,)),
            pltpu.SemaphoreType.DMA((channels // 8,)),
        ],
        name="pack_taps",
    )(late, view)


def pack_kernel(src_ref, out_ref):
    channels, length = src_ref.shape
    rows = length // LANES
    for group in range(channels // 8):
        for row in range(rows):
            value = src_ref[pl.ds(8 * group, 8), pl.ds(row * LANES, LANES)].astype(F32)
            out_ref[pl.ds(8 * group * rows + row, 8, stride=rows), :] = value


def pack(values):
    channels, length = values.shape
    block = 16
    rows = length // LANES
    return pl.pallas_call(
        pack_kernel,
        grid=(channels // block,),
        in_specs=[pl.BlockSpec((block, length), lambda i: (i, 0))],
        out_specs=pl.BlockSpec((block * rows, LANES), lambda i: (i, 0)),
        out_shape=jax.ShapeDtypeStruct((channels * rows, LANES), F32),
        name="pack",
    )(values)


def gate_kernel(conv_ref, signal_ref, gate_ref, skip_ref, out_ref, out, out_sems):
    channels, rows = conv_ref.shape[:2]
    stores = []
    for g in range(channels // 8):
        lines = pl.ds(8 * g, 8)
        skip = skip_ref[lines, :]

        def some(step, carry, g=g, lines=lines, skip=skip):
            for part in range(2):
                base = step * 16 + 8 * part
                tiles = [conv_ref[8 * g + c, pl.ds(pl.multiple_of(base, 8), 8), :] for c in range(8)]
                tiles = swap_eight(tiles)
                for i in range(8):
                    where = (lines, pl.ds(pl.multiple_of((base + i) * LANES, LANES), LANES))
                    total = tiles[i] + skip * signal_ref[where].astype(F32)
                    out[where] = (gate_ref[where].astype(F32) * total).astype(BF16)
            return carry

        lax.fori_loop(0, rows // 16, some, 0)
        if g % 2:
            pair = pl.ds(8 * g - 8, 16)
            stores.append(pltpu.make_async_copy(out.at[pair, :], out_ref.at[pair, :], out_sems.at[g // 2]))
            stores[-1].start()
    for store in stores:
        store.wait()


def gate(conv, signal, gate_values, skip):
    channels, length = signal.shape
    vmem = pl.BlockSpec(memory_space=pltpu.VMEM)
    return pl.pallas_call(
        gate_kernel,
        in_specs=[vmem] * 4,
        out_specs=HBM,
        out_shape=jax.ShapeDtypeStruct((channels, length), BF16),
        scratch_shapes=[
            pltpu.VMEM((channels, length), BF16),
            pltpu.SemaphoreType.DMA((channels // 16,)),
        ],
        compiler_params=pltpu.CompilerParams(vmem_limit_bytes=16 << 20),
        name="gate",
    )(conv, signal, gate_values, skip)


def forward_rows(src, loads, first_hi, first_lo, twist, turn_re, turn_im, work_re, work_im, exact):
    turn_re[...] = twist[0]
    turn_im[...] = twist[1]

    def step(pair, carry):
        for side in range(2):
            loads(2 * pair + side).wait()
        values = jnp.concatenate([src[2 * pair].reshape(ROWS, LANES), src[2 * pair + 1].reshape(ROWS, LANES)], axis=1)
        if exact:
            upper = values.astype(BF16)
            out = dot(first_hi[...], upper) + dot(first_lo[...], upper)
        else:
            upper, lower = split(values)
            out = dot(first_hi[...], upper) + (dot(first_lo[...], upper) + dot(first_hi[...], lower))
        turned = (turn_re[...], turn_im[...])
        for side in range(2):
            lanes = slice(side * LANES, (side + 1) * LANES)
            re, im = times((out[:ROWS, lanes], out[ROWS:, lanes]), turned)
            work_re[2 * pair + side] = re
            work_im[2 * pair + side] = im
            turned = times(turned, (twist[2], twist[3]))
        turn_re[...] = turned[0]
        turn_im[...] = turned[1]
        return carry

    lax.fori_loop(0, MIDS // 2, step, 0)


def forward_mids(mid_ref, work_re, work_im, base, out_re, out_im, place):
    rows, to = pl.ds(base, 8), pl.ds(place, 8)
    out = sixteen_point([(work_re[m, rows], work_im[m, rows]) for m in range(MIDS)], -1)
    for k in range(MIDS):
        value = out[k]
        if k:
            value = times(value, (mid_ref[0, k : k + 1], mid_ref[1, k : k + 1]))
        out_re[k, to] = value[0]
        out_im[k, to] = value[1]


def inverse_mids(mid_ref, twist, work_re, work_im, place, out_re, out_im, base):
    rows, to = pl.ds(place, 8), pl.ds(base, 8)
    values = []
    for k in range(MIDS):
        value = (work_re[k, rows], work_im[k, rows])
        if k:
            value = conj_times(value, (mid_ref[0, k : k + 1], mid_ref[1, k : k + 1]))
        values.append(value)
    out = sixteen_point(values, 1)
    turned = (twist[0, to], twist[1, to])
    step = (twist[2, to], twist[3, to])
    for m in range(MIDS):
        re, im = conj_times(out[m], turned)
        out_re[m, to] = re
        out_im[m, to] = im
        if m + 1 < MIDS:
            turned = times(turned, step)


def lane_stage(values, third_hi, third_lo):
    upper, lower = split(values)
    rows = values.shape[0]
    both = dot(jnp.concatenate([upper, lower], axis=0), third_hi[...])
    return both[:rows] + (both[rows:] + dot(upper, third_lo[...]))


def column(src_ref, buf, sems):
    return lambda m: pltpu.make_async_copy(src_ref.at[:, :, m, :], buf.at[m], sems.at[m])


def taps_kernel(
    src_ref, first_hi, first_lo, third_hi, third_lo, mid_ref, twist, out_ref,
    src, turn_re, turn_im, work_re, work_im, sems,
):
    loads = column(src_ref, src, sems)
    for m in range(MIDS):
        loads(m).start()
    forward_rows(src, loads, first_hi, first_lo, twist, turn_re, turn_im, work_re, work_im, False)

    def mids(group, carry):
        base = pl.multiple_of(group * 8, 8)
        forward_mids(mid_ref, work_re, work_im, base, work_re, work_im, base)
        return carry

    lax.fori_loop(0, ROWS // 8, mids, 0)

    def step(j, carry):
        rows = pl.ds(pl.multiple_of(j * BLOCK, BLOCK), BLOCK)
        parts = [work[:, rows, :].reshape(MIDS * BLOCK, LANES) for work in (work_re, work_im)]
        seen = lane_stage(jnp.concatenate(parts, axis=1), third_hi, third_lo)
        out_ref[:, rows, :] = seen.reshape(MIDS, BLOCK, 2 * LANES)
        return carry

    lax.fori_loop(0, ROWS // BLOCK, step, 0)


SMALL = ("first_hi", "first_lo", "back", "third_hi", "third_lo", "undo_hi", "undo_lo", "mid", "twist")


def convolve_kernel(src_ref, spec_ref, *refs):
    count = len(SMALL)
    tables, out_ref, scratch = refs[:count], refs[count], refs[count + 1 :]
    local, (src, spec, out, turn_re, turn_im, work_re, work_im, done_re, done_im) = scratch[:count], scratch[count : count + 9]
    blocks = [scratch[count + 9 + 4 * i : count + 13 + 4 * i] for i in range(2)]
    sems, table_sems, spec_sem, out_sems = scratch[count + 17 :]
    tab = dict(zip(SMALL, local))
    loads = column(src_ref, src, sems)
    table_loads = {
        name: pltpu.make_async_copy(tables[i], local[i], table_sems.at[i]) for i, name in enumerate(SMALL)
    }
    spec_load = pltpu.make_async_copy(spec_ref, spec, spec_sem)
    early = ("first_hi", "first_lo", "twist")
    for name in early:
        table_loads[name].start()
    for m in range(MIDS):
        loads(m).start()
    for name in SMALL:
        if name not in early:
            table_loads[name].start()
    spec_load.start()
    for name in early:
        table_loads[name].wait()
    forward_rows(src, loads, tab["first_hi"], tab["first_lo"], tab["twist"], turn_re, turn_im, work_re, work_im, True)
    for name in SMALL:
        if name not in early:
            table_loads[name].wait()
    spec_load.wait()
    mid, twist = tab["mid"], tab["twist"]

    def forward(j):
        for g in range(BLOCK // 8):
            forward_mids(mid, work_re, work_im, j * BLOCK + 8 * g, blocks[j % 2][0], blocks[j % 2][1], 8 * g)

    def backward(j):
        for g in range(BLOCK // 8):
            inverse_mids(mid, twist, blocks[j % 2][2], blocks[j % 2][3], 8 * g, done_re, done_im, j * BLOCK + 8 * g)

    def lanes(j):
        in_re, in_im, out_re, out_im = blocks[j % 2]
        rows = MIDS * BLOCK
        values = jnp.concatenate([in_re[...].reshape(rows, LANES), in_im[...].reshape(rows, LANES)], axis=1)
        seen = lane_stage(values, tab["third_hi"], tab["third_lo"])
        wave_h = spec[:, pl.ds(j * BLOCK, BLOCK), :].reshape(rows, 2 * LANES)
        prod = times((seen[:, :LANES], seen[:, LANES:]), (wave_h[:, :LANES], wave_h[:, LANES:]))
        back = lane_stage(jnp.concatenate(prod, axis=1), tab["undo_hi"], tab["undo_lo"])
        out_re[...] = back[:, :LANES].reshape(MIDS, BLOCK, LANES)
        out_im[...] = back[:, LANES:].reshape(MIDS, BLOCK, LANES)

    steps = ROWS // BLOCK
    forward(0)
    for j in range(steps):
        lanes(j)
        if j + 1 < steps:
            forward(j + 1)
        if j:
            backward(j - 1)
    backward(steps - 1)

    def store(m):
        return pltpu.make_async_copy(out.at[m], out_ref.at[:, :, m, :], out_sems.at[m])

    def last(pair, carry):
        values = jnp.concatenate(
            [
                jnp.concatenate([done_re[2 * pair], done_im[2 * pair]], axis=0),
                jnp.concatenate([done_re[2 * pair + 1], done_im[2 * pair + 1]], axis=0),
            ],
            axis=1,
        )
        upper, lower = split(values)
        both = dot(tab["back"][...], upper)
        result = both[:ROWS] + (both[ROWS:] + dot(tab["back"][:ROWS], lower))
        for side in range(2):
            out[2 * pair + side] = result[:, side * LANES : (side + 1) * LANES].reshape(out.shape[1:])
            store(2 * pair + side).start()
        return carry

    lax.fori_loop(0, MIDS // 2, last, 0)
    for m in range(MIDS):
        store(m).wait()


def tables():
    first, third, mid, twist = host_tables()
    first_hi, first_lo = halves_of(first)
    back_hi, back_lo = halves_of(first.T.copy())
    third_hi, third_lo = halves_of(third)
    undo_hi, undo_lo = halves_of(third.T.copy() / TOTAL)
    return dict(
        first_hi=first_hi, first_lo=first_lo, back=np.concatenate([back_hi, back_lo], axis=0),
        third_hi=third_hi, third_lo=third_lo, undo_hi=undo_hi, undo_lo=undo_lo, mid=mid, twist=twist,
    )


def column_scratch(blocks):
    return pltpu.VMEM((MIDS, blocks, ROWS // blocks, LANES), F32)


def transform_taps(taps, tab):
    names = ("first_hi", "first_lo", "third_hi", "third_lo", "mid", "twist")
    vmem = pl.BlockSpec(memory_space=pltpu.VMEM)
    return pl.pallas_call(
        taps_kernel,
        in_specs=[vmem] + [vmem] * len(names),
        out_shape=jax.ShapeDtypeStruct((MIDS, ROWS, 2 * LANES), F32),
        scratch_shapes=[column_scratch(taps.shape[0])]
        + [pltpu.VMEM((ROWS, LANES), F32)] * 2
        + [pltpu.VMEM((MIDS, ROWS, LANES), F32)] * 2
        + [pltpu.SemaphoreType.DMA((MIDS,))],
        compiler_params=pltpu.CompilerParams(vmem_limit_bytes=52 << 20),
        name="taps",
    )(taps, *(tab[n] for n in names))


def convolve(values, spectrum, tab):
    small = [tab[n] for n in SMALL]
    column_buf = column_scratch(values.shape[0])
    whole = pltpu.VMEM((MIDS, ROWS, LANES), F32)
    part = pltpu.VMEM((MIDS, BLOCK, LANES), F32)
    return pl.pallas_call(
        convolve_kernel,
        in_specs=[ANY] + [HBM] * (1 + len(small)),
        out_specs=HBM,
        out_shape=jax.ShapeDtypeStruct(values.shape, F32),
        scratch_shapes=[pltpu.VMEM(t.shape, t.dtype) for t in small]
        + [column_buf, pltpu.VMEM(spectrum.shape, F32), column_buf]
        + [pltpu.VMEM((ROWS, LANES), F32)] * 2
        + [whole] * 4
        + [part] * 8
        + [
            pltpu.SemaphoreType.DMA((MIDS,)),
            pltpu.SemaphoreType.DMA((len(small),)),
            pltpu.SemaphoreType.DMA(()),
            pltpu.SemaphoreType.DMA((MIDS,)),
        ],
        compiler_params=pltpu.CompilerParams(vmem_limit_bytes=58 << 20),
        name="convolve",
    )(values, spectrum, *small)


def shards(signal, filter_taps, gate_values, skip_gain):
    channels, length = signal.shape
    blocks = lax.axis_size("ctx")
    shape = (blocks, ROWS // blocks, MIDS, LANES)
    tab = {k: jnp.asarray(v) for k, v in tables().items()}

    late = (lax.axis_index("ch") % 2).astype(jnp.int32).reshape(1)

    def exchange(values):
        return lax.all_to_all(values.reshape(shape), "ctx", split_axis=0, concat_axis=0, tiled=True)

    taps = pltpu.with_memory_space_constraint(exchange(pack_taps(filter_taps, late)), pltpu.VMEM)
    skip = jnp.broadcast_to(skip_gain[:, None], (channels, LANES))
    packed, skip = lax.optimization_barrier((pack(signal), skip))
    values = exchange(packed)
    spectrum = transform_taps(taps, tab)
    conv = convolve(values, spectrum, tab)
    back = pltpu.with_memory_space_constraint(exchange(conv).reshape(channels, length // LANES, LANES), pltpu.VMEM)
    return gate(back, signal, gate_values, skip)


def solution(mesh):
    in_specs = (P("ch", "ctx"), P("ch", "ctx"), P("ch", "ctx"), P("ch"))
    out_specs = P("ch", "ctx")
    return jax.shard_map(shards, mesh=mesh, in_specs=in_specs, out_specs=out_specs, check_vma=False)
```

```python
import math

import jax
import jax.numpy as jnp
import numpy as np
from jax import lax
from jax.experimental import pallas as pl
from jax.experimental.pallas import tpu as pltpu
from jax.sharding import PartitionSpec as P

F32 = jnp.float32
BF16 = jnp.bfloat16
ROWS = 256
MIDS = 16
LANES = 128
TOTAL = ROWS * MIDS * LANES


def wave(product, period):
    angle = 2.0 * np.pi * (product % period) / period
    return np.cos(angle), np.sin(angle)


def halves_of(table):
    upper = table.astype(jnp.bfloat16)
    lower = (table - upper.astype(np.float64)).astype(jnp.bfloat16)
    return upper, lower


def host_tables():
    n1 = np.arange(ROWS, dtype=np.int64)
    k1 = np.arange(ROWS, dtype=np.int64)
    cos1, sin1 = wave((4 * k1[:, None] + 1) * n1[None, :], 4 * ROWS)
    first = np.concatenate([cos1, -sin1], axis=0)
    lane = np.arange(LANES, dtype=np.int64)
    cos3, sin3 = wave(lane[:, None] * lane[None, :], LANES)
    third = np.block([[cos3, -sin3], [sin3, cos3]])
    k2 = np.arange(MIDS, dtype=np.int64)
    cos2, sin2 = wave(k2[:, None] * lane[None, :], MIDS * LANES)
    mid = np.stack([cos2, -sin2]).astype(np.float32)
    cosp, sinp = wave((4 * k1[:, None] + 1) * lane[None, :], 4 * TOTAL)
    cose, sine = wave(np.broadcast_to((4 * k1[:, None] + 1) * LANES, (ROWS, LANES)), 4 * TOTAL)
    twist = np.stack([cosp, -sinp, cose, -sine]).astype(np.float32)
    return first, third, mid, twist


def split(values):
    upper = values.astype(BF16)
    return upper, (values - upper.astype(F32)).astype(BF16)


def dot(left, right):
    return jnp.dot(left, right, preferred_element_type=F32)


def times(a, b):
    return a[0] * b[0] - a[1] * b[1], a[0] * b[1] + a[1] * b[0]


def conj_times(a, b):
    return a[0] * b[0] + a[1] * b[1], a[1] * b[0] - a[0] * b[1]


def four_point(v, sign):
    s0 = (v[0][0] + v[2][0], v[0][1] + v[2][1])
    d0 = (v[0][0] - v[2][0], v[0][1] - v[2][1])
    s1 = (v[1][0] + v[3][0], v[1][1] + v[3][1])
    d1 = (v[1][0] - v[3][0], v[1][1] - v[3][1])
    r1 = (-sign * d1[1], sign * d1[0]) if sign > 0 else (d1[1], -d1[0])
    return [
        (s0[0] + s1[0], s0[1] + s1[1]),
        (d0[0] + r1[0], d0[1] + r1[1]),
        (s0[0] - s1[0], s0[1] - s1[1]),
        (d0[0] - r1[0], d0[1] - r1[1]),
    ]


def turn(v, step, sign):
    step = step % 16
    if step == 0:
        return v
    root = math.sqrt(0.5)
    if step == 2:
        if sign < 0:
            return ((v[0] + v[1]) * root, (v[1] - v[0]) * root)
        return ((v[0] - v[1]) * root, (v[1] + v[0]) * root)
    if step == 4:
        return (v[1], -v[0]) if sign < 0 else (-v[1], v[0])
    c, s = math.cos(2 * math.pi * step / 16), sign * math.sin(2 * math.pi * step / 16)
    return (v[0] * c - v[1] * s, v[0] * s + v[1] * c)


def sixteen_point(v, sign):
    columns = [four_point([v[4 * p + q] for p in range(4)], sign) for q in range(4)]
    out = [None] * 16
    for r in range(4):
        row = four_point([turn(columns[q][r], q * r, sign) for q in range(4)], sign)
        for s in range(4):
            out[r + 4 * s] = row[s]
    return out


NEAR = LANES // MIDS
STAGGER_NS = 15300
BLOCK = 64
HBM = pl.BlockSpec(memory_space=pltpu.HBM)
ANY = pl.BlockSpec(memory_space=pl.ANY)


def tile_view(values):
    channels, length = values.shape
    return values.reshape(channels // 8, 8, length // LANES, LANES).transpose(0, 2, 1, 3)


def swap_eight(tiles):
    row = lax.broadcasted_iota(jnp.int32, tiles[0].shape, 0)
    tiles = list(tiles)
    for bit in (4, 2, 1):
        odd = (row & bit) != 0
        for low in range(8):
            if low & bit:
                continue
            high = low | bit
            first, second = tiles[low], tiles[high]
            tiles[low] = jnp.where(odd, pltpu.roll(second, bit, 0), first)
            tiles[high] = jnp.where(odd, second, pltpu.roll(first, 8 - bit, 0))
    return tiles


def pack_taps_kernel(late_ref, src_ref, out_ref, buf, lines, in_sems, out_sems):
    groups, rows = src_ref.shape[:2]

    @pl.when(late_ref[0] == 1)
    def _():
        pl.delay(STAGGER_NS)

    loads = [pltpu.make_async_copy(src_ref.at[g], buf.at[g], in_sems.at[g]) for g in range(groups)]
    for load in loads:
        load.start()
    sends = []
    for g in range(groups):
        loads[g].wait()

        def spread(step, carry, g=g):
            for part in range(2):
                base = step * 16 + 8 * part
                tiles = swap_eight([buf[g, base + i] for i in range(8)])
                for c in range(8):
                    lines[8 * g + c, pl.ds(pl.multiple_of(base, 8), 8), :] = tiles[c]
            return carry

        lax.fori_loop(0, rows // 16, spread, 0)
        part = pl.ds(8 * g, 8)
        sends.append(pltpu.make_async_copy(lines.at[part], out_ref.at[part], out_sems.at[g]))
        sends[-1].start()
    for send in sends:
        send.wait()


def pack_taps(values, late):
    channels, length = values.shape
    view = tile_view(values)
    return pl.pallas_call(
        pack_taps_kernel,
        in_specs=[pl.BlockSpec(memory_space=pltpu.SMEM), HBM],
        out_specs=HBM,
        out_shape=jax.ShapeDtypeStruct((channels, length // LANES, LANES), F32),
        scratch_shapes=[
            pltpu.VMEM(view.shape, F32),
            pltpu.VMEM((channels, length // LANES, LANES), F32),
            pltpu.SemaphoreType.DMA((channels // 8,)),
            pltpu.SemaphoreType.DMA((channels // 8,)),
        ],
        name="pack_taps",
    )(late, view)


def pack_kernel(src_ref, out_ref):
    channels, length = src_ref.shape
    rows = length // LANES
    for group in range(channels // 8):
        for row in range(rows):
            value = src_ref[pl.ds(8 * group, 8), pl.ds(row * LANES, LANES)].astype(F32)
            out_ref[pl.ds(8 * group * rows + row, 8, stride=rows), :] = value


def pack(values):
    channels, length = values.shape
    block = 16
    rows = length // LANES
    return pl.pallas_call(
        pack_kernel,
        grid=(channels // block,),
        in_specs=[pl.BlockSpec((block, length), lambda i: (i, 0))],
        out_specs=pl.BlockSpec((block * rows, LANES), lambda i: (i, 0)),
        out_shape=jax.ShapeDtypeStruct((channels * rows, LANES), F32),
        name="pack",
    )(values)


def gate_kernel(conv_ref, signal_ref, gate_ref, skip_ref, out_ref, out, out_sems):
    channels, rows = conv_ref.shape[:2]
    stores = []
    for g in range(channels // 8):
        lines = pl.ds(8 * g, 8)
        skip = skip_ref[lines, :]

        def some(step, carry, g=g, lines=lines, skip=skip):
            for part in range(2):
                base = step * 16 + 8 * part
                tiles = [conv_ref[8 * g + c, pl.ds(pl.multiple_of(base, 8), 8), :] for c in range(8)]
                tiles = swap_eight(tiles)
                for i in range(8):
                    where = (lines, pl.ds(pl.multiple_of((base + i) * LANES, LANES), LANES))
                    total = tiles[i] + skip * signal_ref[where].astype(F32)
                    out[where] = (gate_ref[where].astype(F32) * total).astype(BF16)
            return carry

        lax.fori_loop(0, rows // 16, some, 0)
        if g % 2:
            pair = pl.ds(8 * g - 8, 16)
            stores.append(pltpu.make_async_copy(out.at[pair, :], out_ref.at[pair, :], out_sems.at[g // 2]))
            stores[-1].start()
    for store in stores:
        store.wait()


def gate(conv, signal, gate_values, skip):
    channels, length = signal.shape
    vmem = pl.BlockSpec(memory_space=pltpu.VMEM)
    return pl.pallas_call(
        gate_kernel,
        in_specs=[vmem] * 4,
        out_specs=HBM,
        out_shape=jax.ShapeDtypeStruct((channels, length), BF16),
        scratch_shapes=[
            pltpu.VMEM((channels, length), BF16),
            pltpu.SemaphoreType.DMA((channels // 16,)),
        ],
        compiler_params=pltpu.CompilerParams(vmem_limit_bytes=16 << 20),
        name="gate",
    )(conv, signal, gate_values, skip)


def forward_rows(src, loads, first_hi, first_lo, twist, turn_re, turn_im, work_re, work_im, exact):
    turn_re[...] = twist[0]
    turn_im[...] = twist[1]

    def step(pair, carry):
        for side in range(2):
            loads(2 * pair + side).wait()
        values = jnp.concatenate([src[2 * pair].reshape(ROWS, LANES), src[2 * pair + 1].reshape(ROWS, LANES)], axis=1)
        if exact:
            upper = values.astype(BF16)
            out = dot(first_hi[...], upper) + dot(first_lo[...], upper)
        else:
            upper, lower = split(values)
            out = dot(first_hi[...], upper) + (dot(first_lo[...], upper) + dot(first_hi[...], lower))
        turned = (turn_re[...], turn_im[...])
        for side in range(2):
            lanes = slice(side * LANES, (side + 1) * LANES)
            re, im = times((out[:ROWS, lanes], out[ROWS:, lanes]), turned)
            work_re[2 * pair + side] = re
            work_im[2 * pair + side] = im
            turned = times(turned, (twist[2], twist[3]))
        turn_re[...] = turned[0]
        turn_im[...] = turned[1]
        return carry

    lax.fori_loop(0, MIDS // 2, step, 0)


def forward_mids(mid_ref, work_re, work_im, base, out_re, out_im, place):
    rows, to = pl.ds(base, 8), pl.ds(place, 8)
    out = sixteen_point([(work_re[m, rows], work_im[m, rows]) for m in range(MIDS)], -1)
    for k in range(MIDS):
        value = out[k]
        if k:
            value = times(value, (mid_ref[0, k : k + 1], mid_ref[1, k : k + 1]))
        out_re[k, to] = value[0]
        out_im[k, to] = value[1]


def inverse_mids(mid_ref, twist, work_re, work_im, place, out_re, out_im, base):
    rows, to = pl.ds(place, 8), pl.ds(base, 8)
    values = []
    for k in range(MIDS):
        value = (work_re[k, rows], work_im[k, rows])
        if k:
            value = conj_times(value, (mid_ref[0, k : k + 1], mid_ref[1, k : k + 1]))
        values.append(value)
    out = sixteen_point(values, 1)
    turned = (twist[0, to], twist[1, to])
    step = (twist[2, to], twist[3, to])
    for m in range(MIDS):
        re, im = conj_times(out[m], turned)
        out_re[m, to] = re
        out_im[m, to] = im
        if m + 1 < MIDS:
            turned = times(turned, step)


def lane_stage(values, third_hi, third_lo):
    upper, lower = split(values)
    rows = values.shape[0]
    both = dot(jnp.concatenate([upper, lower], axis=0), third_hi[...])
    return both[:rows] + (both[rows:] + dot(upper, third_lo[...]))


def column(src_ref, buf, sems):
    return lambda m: pltpu.make_async_copy(src_ref.at[:, :, m, :], buf.at[m], sems.at[m])


def taps_kernel(
    src_ref, first_hi, first_lo, third_hi, third_lo, mid_ref, twist, out_ref,
    src, turn_re, turn_im, work_re, work_im, sems,
):
    loads = column(src_ref, src, sems)
    for m in range(MIDS):
        loads(m).start()
    forward_rows(src, loads, first_hi, first_lo, twist, turn_re, turn_im, work_re, work_im, False)

    def mids(group, carry):
        base = pl.multiple_of(group * 8, 8)
        forward_mids(mid_ref, work_re, work_im, base, work_re, work_im, base)
        return carry

    lax.fori_loop(0, ROWS // 8, mids, 0)

    def step(j, carry):
        rows = pl.ds(pl.multiple_of(j * BLOCK, BLOCK), BLOCK)
        parts = [work[:, rows, :].reshape(MIDS * BLOCK, LANES) for work in (work_re, work_im)]
        seen = lane_stage(jnp.concatenate(parts, axis=1), third_hi, third_lo)
        out_ref[:, rows, :] = seen.reshape(MIDS, BLOCK, 2 * LANES)
        return carry

    lax.fori_loop(0, ROWS // BLOCK, step, 0)


SMALL = ("first_hi", "first_lo", "back", "third_hi", "third_lo", "undo_hi", "undo_lo", "mid", "twist")


def convolve_kernel(src_ref, spec_ref, *refs):
    count = len(SMALL)
    tables, out_ref, scratch = refs[:count], refs[count], refs[count + 1 :]
    local, (src, spec, out, turn_re, turn_im, work_re, work_im, done_re, done_im) = scratch[:count], scratch[count : count + 9]
    blocks = [scratch[count + 9 + 4 * i : count + 13 + 4 * i] for i in range(2)]
    sems, table_sems, spec_sem, out_sems = scratch[count + 17 :]
    tab = dict(zip(SMALL, local))
    loads = column(src_ref, src, sems)
    table_loads = {
        name: pltpu.make_async_copy(tables[i], local[i], table_sems.at[i]) for i, name in enumerate(SMALL)
    }
    spec_load = pltpu.make_async_copy(spec_ref, spec, spec_sem)
    early = ("first_hi", "first_lo", "twist")
    for name in early:
        table_loads[name].start()
    for m in range(MIDS):
        loads(m).start()
    for name in SMALL:
        if name not in early:
            table_loads[name].start()
    spec_load.start()
    for name in early:
        table_loads[name].wait()
    forward_rows(src, loads, tab["first_hi"], tab["first_lo"], tab["twist"], turn_re, turn_im, work_re, work_im, True)
    for name in SMALL:
        if name not in early:
            table_loads[name].wait()
    spec_load.wait()
    mid, twist = tab["mid"], tab["twist"]

    def forward(j):
        for g in range(BLOCK // 8):
            forward_mids(mid, work_re, work_im, j * BLOCK + 8 * g, blocks[j % 2][0], blocks[j % 2][1], 8 * g)

    def backward(j):
        for g in range(BLOCK // 8):
            inverse_mids(mid, twist, blocks[j % 2][2], blocks[j % 2][3], 8 * g, done_re, done_im, j * BLOCK + 8 * g)

    def lanes(j):
        in_re, in_im, out_re, out_im = blocks[j % 2]
        rows = MIDS * BLOCK
        values = jnp.concatenate([in_re[...].reshape(rows, LANES), in_im[...].reshape(rows, LANES)], axis=1)
        seen = lane_stage(values, tab["third_hi"], tab["third_lo"])
        wave_h = spec[:, pl.ds(j * BLOCK, BLOCK), :].reshape(rows, 2 * LANES)
        prod = times((seen[:, :LANES], seen[:, LANES:]), (wave_h[:, :LANES], wave_h[:, LANES:]))
        back = lane_stage(jnp.concatenate(prod, axis=1), tab["undo_hi"], tab["undo_lo"])
        out_re[...] = back[:, :LANES].reshape(MIDS, BLOCK, LANES)
        out_im[...] = back[:, LANES:].reshape(MIDS, BLOCK, LANES)

    steps = ROWS // BLOCK
    forward(0)
    for j in range(steps):
        lanes(j)
        if j + 1 < steps:
            forward(j + 1)
        if j:
            backward(j - 1)
    backward(steps - 1)

    def store(m):
        return pltpu.make_async_copy(out.at[m], out_ref.at[:, :, m, :], out_sems.at[m])

    def last(pair, carry):
        values = jnp.concatenate(
            [
                jnp.concatenate([done_re[2 * pair], done_im[2 * pair]], axis=0),
                jnp.concatenate([done_re[2 * pair + 1], done_im[2 * pair + 1]], axis=0),
            ],
            axis=1,
        )
        upper, lower = split(values)
        both = dot(tab["back"][...], upper)
        result = both[:ROWS] + (both[ROWS:] + dot(tab["back"][:ROWS], lower))
        for side in range(2):
            out[2 * pair + side] = result[:, side * LANES : (side + 1) * LANES].reshape(out.shape[1:])
            store(2 * pair + side).start()
        return carry

    lax.fori_loop(0, MIDS // 2, last, 0)
    for m in range(MIDS):
        store(m).wait()


def tables():
    first, third, mid, twist = host_tables()
    first_hi, first_lo = halves_of(first)
    back_hi, back_lo = halves_of(first.T.copy())
    third_hi, third_lo = halves_of(third)
    undo_hi, undo_lo = halves_of(third.T.copy() / TOTAL)
    return dict(
        first_hi=first_hi, first_lo=first_lo, back=np.concatenate([back_hi, back_lo], axis=0),
        third_hi=third_hi, third_lo=third_lo, undo_hi=undo_hi, undo_lo=undo_lo, mid=mid, twist=twist,
    )


def column_scratch(blocks):
    return pltpu.VMEM((MIDS, blocks, ROWS // blocks, LANES), F32)


def transform_taps(taps, tab):
    names = ("first_hi", "first_lo", "third_hi", "third_lo", "mid", "twist")
    vmem = pl.BlockSpec(memory_space=pltpu.VMEM)
    return pl.pallas_call(
        taps_kernel,
        in_specs=[vmem] + [vmem] * len(names),
        out_shape=jax.ShapeDtypeStruct((MIDS, ROWS, 2 * LANES), F32),
        scratch_shapes=[column_scratch(taps.shape[0])]
        + [pltpu.VMEM((ROWS, LANES), F32)] * 2
        + [pltpu.VMEM((MIDS, ROWS, LANES), F32)] * 2
        + [pltpu.SemaphoreType.DMA((MIDS,))],
        compiler_params=pltpu.CompilerParams(vmem_limit_bytes=52 << 20),
        name="taps",
    )(taps, *(tab[n] for n in names))


def convolve(values, spectrum, tab):
    small = [tab[n] for n in SMALL]
    column_buf = column_scratch(values.shape[0])
    whole = pltpu.VMEM((MIDS, ROWS, LANES), F32)
    part = pltpu.VMEM((MIDS, BLOCK, LANES), F32)
    return pl.pallas_call(
        convolve_kernel,
        in_specs=[ANY] + [HBM] * (1 + len(small)),
        out_specs=HBM,
        out_shape=jax.ShapeDtypeStruct(values.shape, F32),
        scratch_shapes=[pltpu.VMEM(t.shape, t.dtype) for t in small]
        + [column_buf, pltpu.VMEM(spectrum.shape, F32), column_buf]
        + [pltpu.VMEM((ROWS, LANES), F32)] * 2
        + [whole] * 4
        + [part] * 8
        + [
            pltpu.SemaphoreType.DMA((MIDS,)),
            pltpu.SemaphoreType.DMA((len(small),)),
            pltpu.SemaphoreType.DMA(()),
            pltpu.SemaphoreType.DMA((MIDS,)),
        ],
        compiler_params=pltpu.CompilerParams(vmem_limit_bytes=58 << 20),
        name="convolve",
    )(values, spectrum, *small)


def shards(signal, filter_taps, gate_values, skip_gain):
    channels, length = signal.shape
    blocks = lax.axis_size("ctx")
    shape = (blocks, ROWS // blocks, MIDS, LANES)
    tab = {k: jnp.asarray(v) for k, v in tables().items()}

    late = (lax.axis_index("ch") % 2).astype(jnp.int32).reshape(1)

    def exchange(values):
        return lax.all_to_all(values.reshape(shape), "ctx", split_axis=0, concat_axis=0, tiled=True)

    taps = pltpu.with_memory_space_constraint(exchange(pack_taps(filter_taps, late)), pltpu.VMEM)
    skip = jnp.broadcast_to(skip_gain[:, None], (channels, LANES))
    packed, skip = lax.optimization_barrier((pack(signal), skip))
    values = exchange(packed)
    spectrum = transform_taps(taps, tab)
    conv = convolve(values, spectrum, tab)
    back = pltpu.with_memory_space_constraint(exchange(conv).reshape(channels, length // LANES, LANES), pltpu.VMEM)
    return gate(back, signal, gate_values, skip)


def solution(mesh):
    in_specs = (P("ch", "ctx"), P("ch", "ctx"), P("ch", "ctx"), P("ch"))
    out_specs = P("ch", "ctx")
    return jax.shard_map(shards, mesh=mesh, in_specs=in_specs, out_specs=out_specs, check_vma=False)
```
